32 devices in a mesh: expert: 4 (over y, x), shard: 8 (over z, core).
Axes of the slice: x: 2, y: 2, z: 4, core: 2. Of those that a mesh axis runs over, the one named last changes fastest.
Arguments:
- inputs: bfloat16 [4096, 1536], P(('expert', 'shard')), may hold values from -6 to 6
- lengths: int32 [4, 3], P('expert'), may hold values from 1 to 512, 1024 in all within a row
- routes: int32 [4096, 8], P(('expert', 'shard')), may hold values from 0 to 39, all different within a row; in each aligned block of 128 rows (0 to 127, 128 to 255, ...) at most 32 rows name the same one
- gain_attn: bfloat16 [1536], P(('expert', 'shard')), may hold values from 0.5 to 1.5
- w_query: bfloat16 [1536, 1536], P(('expert', 'shard')), may hold values from -0.15625 to 0.15625
- key_weight: bfloat16 [1536, 512], P(('expert', 'shard')), may hold values from -0.15625 to 0.15625
- value_weight: bfloat16 [1536, 512], P(('expert', 'shard')), may hold values from -0.15625 to 0.15625
- w_out: bfloat16 [1536, 1536], P(('expert', 'shard')), may hold values from -0.625 to 0.625
- gain_ffn: bfloat16 [1536], P(('expert', 'shard')), may hold values from 0.5 to 1.5
- w_router: bfloat16 [1536, 40], P(('expert', 'shard')), may hold values from -0.0390625 to 0.0390625
- w_gate: bfloat16 [40, 1536, 512], P('expert', 'shard'), may hold values from -0.15625 to 0.15625
- w_up: bfloat16 [40, 1536, 512], P('expert', 'shard'), may hold values from -0.15625 to 0.15625
- w_down: bfloat16 [40, 512, 1536], P('expert', 'shard'), may hold values from -0.25 to 0.25
- cotangent: bfloat16 [4096, 1536], P(('expert', 'shard')), may hold values from -6 to 6
Outputs:
- output: bfloat16 [4096, 1536], P(('expert', 'shard'))
- input_grad: float32 [4096, 1536], P(('expert', 'shard'))
- gain_attn_grad: float32 [1536], P(('expert', 'shard'))
- query_grad: float32 [1536, 1536], P(('expert', 'shard'))
- key_grad: float32 [1536, 512], P(('expert', 'shard'))
- value_grad: float32 [1536, 512], P(('expert', 'shard'))
- out_grad: float32 [1536, 1536], P(('expert', 'shard'))
- gain_ffn_grad: float32 [1536], P(('expert', 'shard'))
- router_grad: float32 [1536, 40], P(('expert', 'shard'))
- gate_grad: float32 [40, 1536, 512], P('expert', 'shard')
- up_grad: float32 [40, 1536, 512], P('expert', 'shard')
- down_grad: float32 [40, 512, 1536], P('expert', 'shard')
The draws below stay inside these ranges and needn't reach their ends.
Inputs may be any that keep to these rules, and one draw needn't show every extreme that they name: `routes`: in each aligned block of 128 rows (the rows of one device) no expert is named by more than 32 rows, a bound that some block reaches; a row names 8 different experts. `lengths`: each row sums to 1024 and its largest entry is 512.
All inputs are finite; a program needn't handle non-finite values.
Results may differ from the reference program's by a relative error of at most 0.017.
Values may be sent and summed in bfloat16 or wider, within the bound.
No kernel may reach another device: no remote copies, remote signals or barrier semaphores. Data moves between devices by JAX's collectives and lax.ppermute only.
A program may use at most 320 MiB of HBM per device.

```python
import math
import jax
import jax.numpy as jnp
import numpy as np
from jax import lax

MODEL_DIMENSION = 1536
QUERY_HEADS = 24
KEY_VALUE_HEADS = 8
HEAD_SIZE = 64
FF = 512
TOP = 8
TOK_DEV = 128
EXPERTS = 40
CAP = 32
GROUP = 1024
MAXLEN = 512
SEQS = 3
TOKENS = 4096
N_EXPERT = 4
N_SHARD = 8
DEVICES = 32


def levels(own_key, dims, pieces, least, high):
    level = 1.0
    for position, blocks in pieces:
        steps = jax.random.uniform(jax.random.fold_in(jax.random.fold_in(own_key, 6), position), (blocks,), jnp.float32, least / len(pieces), high / len(pieces))
        level = level * jnp.repeat(jnp.exp(steps), dims[position] // blocks).reshape((-1,) + (1,) * (len(dims) - 1 - position))
    return level


def split_up(number_of, total, limit, lean):
    weights = [(1 << 20) // math.isqrt(grade ** lean) + 1 for grade in range(2, number_of + 1)]
    surplus, holding = total - limit - (number_of - 1), [1] * (number_of - 1)
    while surplus > 0:
        free = [i for i in range(number_of - 1) if holding[i] < limit]
        mass, remaining = sum([weights[i] for i in free]), surplus
        for i in free:
            extra = min(limit - holding[i], max(1, remaining * weights[i] // mass), surplus)
            holding[i] = holding[i] + extra
            surplus = surplus - extra
    return np.array([limit] + holding)


def uneven(key, number_of, total, limit, slope):
    if number_of == 2:
        one = jax.random.randint(key, (), max(1, total - limit), min(limit, total - 1) + 1)
        return jnp.stack([one, total - one])
    sizes = jnp.asarray(split_up(number_of, total, limit, slope), jnp.int32)
    pairs = (number_of - 1) // 2
    source_of, taker = sizes[1:1 + 2 * pairs:2], sizes[2:2 + 2 * pairs:2]
    room = jnp.minimum(source_of - 1, limit - taker)
    passed = jax.random.randint(jax.random.fold_in(key, 1), (pairs,), 0, 1 << 20) % (room + 1)
    sizes = sizes.at[1:1 + 2 * pairs:2].set(source_of - passed).at[2:2 + 2 * pairs:2].set(taker + passed)
    return sizes[jax.random.permutation(jax.random.fold_in(key, 2), number_of)]


def assign_block(key, own, number, rows, count, top, limit, lean):
    ranking = jax.random.permutation(key, count)
    packed, common = shares(count, rows * top, limit, lean, True), shares(count, rows * top, limit, lean, False)
    places = jnp.arange(count)

    def named(sizes, rotation):
        used = int((sizes > 0).sum())
        fixed = max(1, used // 4)
        passed = fixed + (places - fixed + rotation * (used - fixed)) % max(1, count - fixed)
        return jnp.zeros((count,), jnp.int32).at[ranking[jnp.where(places < fixed, places, passed)]].set(jnp.asarray(sizes, jnp.int32))

    sizes = jnp.where(number % 4 == 0, named(packed, number // 4), named(common, number - number // 4 - 1))
    mixed = jax.random.permutation(jax.random.fold_in(own, 3), count)
    donor, receiver = mixed[0:count // 2 * 2:2], mixed[1:count // 2 * 2:2]
    margin = jnp.minimum(sizes[donor] - 1, limit - sizes[receiver]) // 2
    margin = jnp.where((donor == ranking[0]) | (receiver == ranking[0]) | (sizes[receiver] == 0), 0, jnp.maximum(margin, 0))
    passed = jax.random.randint(jax.random.fold_in(own, 4), (count // 2,), 0, 1 << 20) % (margin + 1)
    sizes = sizes.at[donor].add(-passed).at[receiver].add(passed)
    items = jnp.searchsorted(jnp.cumsum(sizes), jnp.arange(rows * top), side="right").astype(jnp.int32)
    grid = items.reshape(top, rows).T
    grid = grid[jax.random.permutation(jax.random.fold_in(own, 1), rows)]
    rotation = jax.random.randint(jax.random.fold_in(own, 2), (rows, 1), 0, top)
    return jnp.take_along_axis(grid, (jnp.arange(top)[None, :] + rotation) % top, axis=1)


def shares(count, total, bound, skew, full):
    portions = [(1 << 20) // math.isqrt(standing ** skew) + 1 for standing in range(1, count + 1)]
    largest = bound if full else min(bound, max(-(-total // count), total * portions[0] // sum(portions)))
    least = 1 if total - largest >= count - 1 else 0
    given, surplus = [largest] + [least] * (count - 1), total - largest - least * (count - 1)
    while surplus > 0:
        movable = [i for i in range(1, count) if given[i] < largest] or [i for i in range(1, count) if given[i] < bound]
        whole, budget = sum([portions[i] for i in movable]), surplus
        for i in movable:
            more = min(bound - given[i], max(1, budget * portions[i] // whole), surplus)
            given[i] = given[i] + more
            surplus = surplus - more
    return np.array(given)


def gaussian(own_key, extent, spread, limit, shards=(), kind=jnp.bfloat16):
    factor_of = levels(own_key, extent, shards, -0.22, 0.18) if shards else 1.0
    values = jax.random.normal(own_key, extent, jnp.float32) * spread * factor_of
    return jnp.minimum(jnp.maximum(values, -limit), limit).astype(kind)


def setup_inputs(seed: int = 0) -> dict:
    keys = jax.random.split(jax.random.key(seed), 15)
    inputs = gaussian(keys[0], (TOKENS, MODEL_DIMENSION), 1.0, 6.0, ((0, 32),))
    lengths = jax.vmap(lambda own: uneven(own, SEQS, GROUP, MAXLEN, 2))(jax.random.split(keys[1], N_EXPERT)).reshape((N_EXPERT, SEQS)).astype(jnp.int32)
    routes_keys = jax.random.split(jax.random.fold_in(keys[2], 1), TOKENS // TOK_DEV)
    routes_turns = jax.random.permutation(jax.random.fold_in(keys[2], 3), TOKENS // TOK_DEV)
    routes = jax.vmap(lambda own, number: assign_block(jax.random.fold_in(keys[2], 2), own, number, TOK_DEV, EXPERTS, TOP, CAP, 2))(routes_keys, routes_turns).reshape((TOKENS, TOP))
    gain_attn = jnp.clip(1.0 + 0.1 * jax.random.normal(keys[3], (MODEL_DIMENSION,), jnp.float32), 0.5, 1.5).astype(jnp.bfloat16)
    w_query = gaussian(keys[4], (MODEL_DIMENSION, QUERY_HEADS * HEAD_SIZE), MODEL_DIMENSION ** -0.5, 0.15625, ((0, 32),))
    key_weight = gaussian(keys[5], (MODEL_DIMENSION, KEY_VALUE_HEADS * HEAD_SIZE), MODEL_DIMENSION ** -0.5, 0.15625, ((0, 32),))
    value_weight = gaussian(keys[6], (MODEL_DIMENSION, KEY_VALUE_HEADS * HEAD_SIZE), MODEL_DIMENSION ** -0.5, 0.15625, ((0, 32),))
    w_out = gaussian(keys[7], (QUERY_HEADS * HEAD_SIZE, MODEL_DIMENSION), (QUERY_HEADS * HEAD_SIZE // 16) ** -0.5, 0.625, ((0, 32),))
    gain_ffn = jnp.clip(1.0 + 0.1 * jax.random.normal(keys[8], (MODEL_DIMENSION,), jnp.float32), 0.5, 1.5).astype(jnp.bfloat16)
    w_router = gaussian(keys[9], (MODEL_DIMENSION, EXPERTS), (16 * MODEL_DIMENSION) ** -0.5, 0.0390625, ((0, 32),))
    w_gate = gaussian(keys[10], (EXPERTS, MODEL_DIMENSION, FF), MODEL_DIMENSION ** -0.5, 0.15625, ((0, 4), (1, 8)))
    w_up = gaussian(keys[11], (EXPERTS, MODEL_DIMENSION, FF), MODEL_DIMENSION ** -0.5, 0.15625, ((0, 4), (1, 8)))
    w_down = gaussian(keys[12], (EXPERTS, FF, MODEL_DIMENSION), FF ** -0.5, 0.25, ((0, 4), (1, 8)))
    cotangent = gaussian(keys[13], (TOKENS, MODEL_DIMENSION), 1.0, 6.0, ((0, 32),))
    return dict(inputs=inputs, lengths=lengths, routes=routes, gain_attn=gain_attn, w_query=w_query, key_weight=key_weight, value_weight=value_weight, w_out=w_out, gain_ffn=gain_ffn, w_router=w_router, w_gate=w_gate, w_up=w_up, w_down=w_down, cotangent=cotangent)


EPSILON = 1e-05
SCORE_SCALE = 0.125
ROPE_BASE = 10000.0

def apply_rotation(value_rows, positions, head_count, direction_sign):
    head_width = value_rows.shape[1] // head_count
    half_width = head_width // 2
    frequency = ROPE_BASE ** (-jnp.arange(half_width, dtype=jnp.float32) * 2.0 / head_width)
    angles = positions.astype(jnp.float32)[:, None] * frequency[None, :]
    cosine = jnp.cos(angles)[:, None, :]
    sine_part = direction_sign * jnp.sin(angles)[:, None, :]
    shaped = value_rows.reshape(value_rows.shape[0], head_count, head_width)
    first_half = shaped[..., :half_width]
    second_half = shaped[..., half_width:]
    turned = jnp.concatenate([first_half * cosine - second_half * sine_part, second_half * cosine + first_half * sine_part], axis=-1)
    return turned.reshape(value_rows.shape)

def norm_rows(value_rows, gain_row):
    inv_scale = lax.rsqrt(lax.optimization_barrier(jnp.mean(value_rows * value_rows, axis=-1, keepdims=True)) + EPSILON)
    return (value_rows * inv_scale * gain_row, inv_scale)

def norm_back(norm_grad, value_rows, inv_scale, gain_row):
    gain_part = lax.optimization_barrier(jnp.sum(norm_grad * value_rows * inv_scale, axis=0))
    scaled = norm_grad * gain_row
    value_part = inv_scale * scaled - value_rows * inv_scale ** 3 * lax.optimization_barrier(jnp.mean(scaled * value_rows, axis=-1, keepdims=True))
    return (gain_part, value_part)

def split_query(value_rows):
    return value_rows.reshape(value_rows.shape[0], KEY_VALUE_HEADS, QUERY_HEADS // KEY_VALUE_HEADS, HEAD_SIZE).transpose(1, 0, 2, 3)

def split_keys(value_rows):
    return value_rows.reshape(value_rows.shape[0], KEY_VALUE_HEADS, HEAD_SIZE).transpose(1, 0, 2)

def merge_query(value_rows):
    return value_rows.transpose(1, 0, 2, 3).reshape(value_rows.shape[1], QUERY_HEADS * HEAD_SIZE)

def merge_keys(value_rows):
    return value_rows.transpose(1, 0, 2).reshape(value_rows.shape[1], KEY_VALUE_HEADS * HEAD_SIZE)

def widen(value_rows):
    return lax.optimization_barrier(value_rows).astype(jnp.float32)

def attend(queries, keys_win, values_win, allowed):

    def one_head(parts):
        query_head, key_head, value_head = parts
        scores = jnp.einsum('tgd,wd->gtw', widen(query_head), widen(key_head)) * SCORE_SCALE
        scores = jnp.where(allowed[None], scores, -1e+30)
        largest = lax.optimization_barrier(jnp.max(scores, axis=-1, keepdims=True))
        expo_terms = jnp.exp(scores - largest)
        totals = lax.optimization_barrier(jnp.sum(expo_terms, axis=-1, keepdims=True))
        probs_low = (expo_terms / totals).astype(jnp.bfloat16)
        mixed_head = jnp.einsum('gtw,wd->tgd', widen(probs_low), widen(value_head))
        return (mixed_head.astype(jnp.bfloat16), (largest + jnp.log(totals))[..., 0])
    heads_out, log_totals = lax.map(one_head, (split_query(queries), split_keys(keys_win), split_keys(values_win)))
    return (merge_query(heads_out), log_totals)

def attend_back(queries, keys_win, values_win, outputs, out_grads, log_totals, allowed):

    def one_head(parts):
        query_head, key_head, value_head, out_head, grad_head, lse_head = parts
        query_wide = widen(query_head)
        key_wide = widen(key_head)
        grad_wide = widen(grad_head)
        scores = jnp.einsum('tgd,wd->gtw', query_wide, key_wide) * SCORE_SCALE
        scores = jnp.where(allowed[None], scores, -1e+30)
        attn_probs = jnp.exp(scores - lse_head[..., None])
        probs_low = widen(attn_probs.astype(jnp.bfloat16))
        value_part = jnp.einsum('gtw,tgd->wd', probs_low, grad_wide)
        prob_part = jnp.einsum('tgd,wd->gtw', grad_wide, widen(value_head))
        delta_rows = lax.optimization_barrier(jnp.sum(widen(out_head) * grad_wide, axis=-1)).T
        score_grad = widen((attn_probs * (prob_part - delta_rows[..., None]) * SCORE_SCALE).astype(jnp.bfloat16))
        query_part = jnp.einsum('gtw,wd->tgd', score_grad, key_wide)
        key_part = jnp.einsum('gtw,tgd->wd', score_grad, query_wide)
        return (query_part, key_part, value_part)
    parts = (split_query(queries), split_keys(keys_win), split_keys(values_win), split_query(outputs), split_query(out_grads), log_totals)
    query_parts, key_parts, value_parts = lax.map(one_head, parts)
    return (merge_query(query_parts), merge_keys(key_parts), merge_keys(value_parts))

def reference(inputs, lengths, routes, gain_attn, w_query, key_weight, value_weight, w_out, gain_ffn, w_router, w_gate, w_up, w_down, cotangent):
    resid = inputs.astype(jnp.float32)
    token_count = resid.shape[0]
    group_size = token_count // N_EXPERT
    token_index = jnp.arange(token_count, dtype=jnp.int32)
    owner_index = token_index // group_size
    within = token_index % group_size
    token_lengths = lengths[owner_index]
    seq_ends = jnp.cumsum(token_lengths, axis=1)
    seq_starts = lax.optimization_barrier(jnp.sum(jnp.where(seq_ends <= within[:, None], token_lengths, 0), axis=1)).astype(jnp.int32)
    sequence_offsets = within - seq_starts
    attn_gain = gain_attn.astype(jnp.float32)
    ffn_gain = gain_ffn.astype(jnp.float32)
    normed_wide, inv_attn = norm_rows(resid, attn_gain)
    normalized_rows = normed_wide.astype(jnp.bfloat16)
    queries = apply_rotation(jnp.dot(normalized_rows, w_query, preferred_element_type=jnp.float32), sequence_offsets, QUERY_HEADS, 1.0).astype(jnp.bfloat16)
    keys_every_head = apply_rotation(jnp.dot(normalized_rows, key_weight, preferred_element_type=jnp.float32), sequence_offsets, KEY_VALUE_HEADS, 1.0).astype(jnp.bfloat16)
    values_all = jnp.dot(normalized_rows, value_weight, preferred_element_type=jnp.float32).astype(jnp.bfloat16)
    kv_width = keys_every_head.shape[1]
    front_pad = jnp.zeros((N_EXPERT, MAXLEN, kv_width), jnp.bfloat16)
    keys_pad = jnp.concatenate([front_pad, keys_every_head.reshape(N_EXPERT, group_size, kv_width)], axis=1)
    values_pad = jnp.concatenate([front_pad, values_all.reshape(N_EXPERT, group_size, kv_width)], axis=1)
    window_size = TOK_DEV + MAXLEN

    def block_parts(block_id):
        team_id = block_id // N_SHARD
        place_id = block_id % N_SHARD
        query_pos = place_id * TOK_DEV + jnp.arange(TOK_DEV, dtype=jnp.int32)
        query_start = lax.dynamic_slice_in_dim(seq_starts, block_id * TOK_DEV, TOK_DEV, 0)
        key_pos = place_id * TOK_DEV - MAXLEN + jnp.arange(window_size, dtype=jnp.int32)
        allowed = (key_pos[None, :] >= query_start[:, None]) & (key_pos[None, :] <= query_pos[:, None])
        corner = (team_id, place_id * TOK_DEV, jnp.int32(0))
        keys_win = lax.dynamic_slice(keys_pad, corner, (1, window_size, kv_width))[0]
        values_win = lax.dynamic_slice(values_pad, corner, (1, window_size, kv_width))[0]
        return (allowed, keys_win, values_win, corner)

    def forward_block(carry, block_id):
        allowed, keys_win, values_win, corner = block_parts(block_id)
        query_block = lax.dynamic_slice_in_dim(queries, block_id * TOK_DEV, TOK_DEV, 0)
        out_block, lse_block = attend(query_block, keys_win, values_win, allowed)
        return (carry, (out_block, lse_block))
    block_ids = jnp.arange(DEVICES, dtype=jnp.int32)
    _, (attended, log_totals) = lax.scan(forward_block, jnp.int32(0), block_ids)
    attended = attended.reshape(token_count, QUERY_HEADS * HEAD_SIZE)
    hidden = resid + jnp.dot(attended, w_out, preferred_element_type=jnp.float32)
    normed2_wide, inv_ffn = norm_rows(hidden, ffn_gain)
    normed2 = normed2_wide.astype(jnp.bfloat16)
    router_probs = jax.nn.softmax(jnp.dot(normed2, w_router, preferred_element_type=jnp.float32), axis=-1)
    route_weights = jnp.take_along_axis(router_probs, routes, axis=1)
    flat_routes = routes.reshape(-1)
    top_k = routes.shape[1]
    assigned = flat_routes.shape[0]
    flat_weights = route_weights.reshape(-1)
    upstream = cotangent.astype(jnp.float32)
    row_limit = DEVICES * CAP

    def expert_step(carry, parts):
        mix_total, normed2_grad, weight_grads = carry
        expert_id, gate_mat, up_mat, down_mat = parts
        row_index = jnp.nonzero(flat_routes == expert_id, size=row_limit, fill_value=assigned)[0].astype(jnp.int32)
        is_valid = row_index < assigned
        safe_index = jnp.minimum(row_index, assigned - 1)
        token_of = safe_index // top_k
        expert_in = jnp.where(is_valid[:, None], normed2[token_of], jnp.zeros((), jnp.bfloat16))
        gate_pre = jnp.dot(expert_in, gate_mat, preferred_element_type=jnp.float32)
        up_pre = jnp.dot(expert_in, up_mat, preferred_element_type=jnp.float32)
        expert_act = (jax.nn.silu(gate_pre) * up_pre).astype(jnp.bfloat16)
        expert_rows = jnp.dot(expert_act, down_mat, preferred_element_type=jnp.float32).astype(jnp.bfloat16)
        rows_wide = widen(expert_rows)
        row_weight = jnp.where(is_valid, flat_weights[safe_index], 0.0)
        row_upstream = upstream[token_of]
        mix_total = mix_total.at[token_of].add(row_weight[:, None] * rows_wide)
        rows_grad = (row_weight[:, None] * row_upstream).astype(jnp.bfloat16)
        weight_grads = weight_grads.at[row_index].set(lax.optimization_barrier(jnp.sum(row_upstream * rows_wide, axis=-1)), mode='drop')
        down_part = jnp.dot(expert_act.T, rows_grad, preferred_element_type=jnp.float32)
        act_grad = jnp.dot(rows_grad, down_mat.T, preferred_element_type=jnp.float32)
        sigma = jax.nn.sigmoid(gate_pre)
        gate_pre_grad = (act_grad * up_pre * sigma * (1.0 + gate_pre * (1.0 - sigma))).astype(jnp.bfloat16)
        up_pre_grad = (act_grad * gate_pre * sigma).astype(jnp.bfloat16)
        gate_part = jnp.dot(expert_in.T, gate_pre_grad, preferred_element_type=jnp.float32)
        up_part = jnp.dot(expert_in.T, up_pre_grad, preferred_element_type=jnp.float32)
        pair_grad = (jnp.dot(gate_pre_grad, gate_mat.T, preferred_element_type=jnp.float32) + jnp.dot(up_pre_grad, up_mat.T, preferred_element_type=jnp.float32)).astype(jnp.bfloat16)
        normed2_grad = normed2_grad.at[token_of].add(widen(pair_grad))
        return ((mix_total, normed2_grad, weight_grads), (gate_part, up_part, down_part))
    start_carry = (jnp.zeros((token_count, MODEL_DIMENSION), jnp.float32), jnp.zeros((token_count, MODEL_DIMENSION), jnp.float32), jnp.zeros((assigned,), jnp.float32))
    expert_ids = jnp.arange(w_gate.shape[0], dtype=jnp.int32)
    (mix_total, normed2_grad, weight_grads), (gate_grad, up_grad, down_grad) = lax.scan(expert_step, start_carry, (expert_ids, w_gate, w_up, w_down))
    output = (hidden + mix_total).astype(jnp.bfloat16)
    prob_grad = jnp.zeros_like(router_probs).at[token_index[:, None], routes].add(weight_grads.reshape(token_count, top_k))
    logit_grad = (router_probs * (prob_grad - lax.optimization_barrier(jnp.sum(router_probs * prob_grad, axis=-1, keepdims=True)))).astype(jnp.bfloat16)
    router_grad = jnp.dot(normed2.T, logit_grad, preferred_element_type=jnp.float32)
    normed2_grad = normed2_grad + jnp.dot(logit_grad, w_router.T, preferred_element_type=jnp.float32)
    gain_ffn_grad, hidden_part = norm_back(normed2_grad, hidden, inv_ffn, ffn_gain)
    hidden_grad = upstream + hidden_part
    hidden_low = hidden_grad.astype(jnp.bfloat16)
    out_grad = jnp.dot(attended.T, hidden_low, preferred_element_type=jnp.float32)
    attended_grad = jnp.dot(hidden_low, w_out.T, preferred_element_type=jnp.float32).astype(jnp.bfloat16)

    def backward_block(carry, block_id):
        keys_acc, values_acc = carry
        allowed, keys_win, values_win, corner = block_parts(block_id)
        query_block = lax.dynamic_slice_in_dim(queries, block_id * TOK_DEV, TOK_DEV, 0)
        out_block = lax.dynamic_slice_in_dim(attended, block_id * TOK_DEV, TOK_DEV, 0)
        grad_block = lax.dynamic_slice_in_dim(attended_grad, block_id * TOK_DEV, TOK_DEV, 0)
        query_part, key_part, value_part = attend_back(query_block, keys_win, values_win, out_block, grad_block, log_totals[block_id], allowed)
        current_keys = lax.dynamic_slice(keys_acc, corner, (1, window_size, kv_width))
        keys_acc = lax.dynamic_update_slice(keys_acc, current_keys + key_part[None], corner)
        current_values = lax.dynamic_slice(values_acc, corner, (1, window_size, kv_width))
        values_acc = lax.dynamic_update_slice(values_acc, current_values + value_part[None], corner)
        return ((keys_acc, values_acc), query_part)
    acc_zero = jnp.zeros((N_EXPERT, MAXLEN + group_size, kv_width), jnp.float32)
    (keys_acc, values_acc), query_raw = lax.scan(backward_block, (acc_zero, acc_zero), block_ids)
    keys_unrotated = keys_acc[:, MAXLEN:].reshape(token_count, kv_width)
    values_raw = values_acc[:, MAXLEN:].reshape(token_count, kv_width)
    queries_grad = apply_rotation(query_raw.reshape(token_count, QUERY_HEADS * HEAD_SIZE), sequence_offsets, QUERY_HEADS, -1.0).astype(jnp.bfloat16)
    keys_gradient = apply_rotation(keys_unrotated, sequence_offsets, KEY_VALUE_HEADS, -1.0).astype(jnp.bfloat16)
    values_grad = values_raw.astype(jnp.bfloat16)
    query_grad = jnp.dot(normalized_rows.T, queries_grad, preferred_element_type=jnp.float32)
    key_grad = jnp.dot(normalized_rows.T, keys_gradient, preferred_element_type=jnp.float32)
    value_grad = jnp.dot(normalized_rows.T, values_grad, preferred_element_type=jnp.float32)
    normed_grad = jnp.dot(queries_grad, w_query.T, preferred_element_type=jnp.float32) + jnp.dot(keys_gradient, key_weight.T, preferred_element_type=jnp.float32) + jnp.dot(values_grad, value_weight.T, preferred_element_type=jnp.float32)
    gain_attn_grad, input_part = norm_back(normed_grad, resid, inv_attn, attn_gain)
    input_grad = hidden_grad + input_part
    return (output, input_grad, gain_attn_grad, query_grad, key_grad, value_grad, out_grad, gain_ffn_grad, router_grad, gate_grad, up_grad, down_grad)
```

```python
import jax
import jax.numpy as jnp
from jax import lax
from jax.sharding import PartitionSpec as P

QUERY_HEADS = 24
KEY_VALUE_HEADS = 8
HEAD_SIZE = 64
SEQ_MOST = 2048
CAP = 32


EPSILON = 1e-05
SCORE_SCALE = 0.125
ROPE_BASE = 10000.0


def apply_rotation(value_rows, positions, head_count, direction_sign):
    head_width = value_rows.shape[1] // head_count
    half_width = head_width // 2
    frequency = ROPE_BASE ** (-jnp.arange(half_width, dtype=jnp.float32) * 2.0 / head_width)
    angles = positions.astype(jnp.float32)[:, None] * frequency[None, :]
    cosine = jnp.cos(angles)[:, None, :]
    sine_part = direction_sign * jnp.sin(angles)[:, None, :]
    shaped = value_rows.reshape(value_rows.shape[0], head_count, head_width)
    first_half = shaped[..., :half_width]
    second_half = shaped[..., half_width:]
    turned = jnp.concatenate(
        [
            first_half * cosine - second_half * sine_part,
            second_half * cosine + first_half * sine_part,
        ],
        axis=-1,
    )
    return turned.reshape(value_rows.shape)


def norm_rows(value_rows, gain_row):
    inv_scale = lax.rsqrt(jnp.mean(value_rows * value_rows, axis=-1, keepdims=True) + EPSILON)
    return (value_rows * inv_scale * gain_row, inv_scale)


def norm_back(norm_grad, value_rows, inv_scale, gain_row):
    gain_part = jnp.sum(norm_grad * value_rows * inv_scale, axis=0)
    scaled = norm_grad * gain_row
    value_part = inv_scale * scaled - value_rows * inv_scale**3 * jnp.mean(
        scaled * value_rows, axis=-1, keepdims=True
    )
    return (gain_part, value_part)


def split_query(value_rows):
    return value_rows.reshape(
        value_rows.shape[0], KEY_VALUE_HEADS, QUERY_HEADS // KEY_VALUE_HEADS, HEAD_SIZE
    ).transpose(1, 0, 2, 3)


def split_keys(value_rows):
    return value_rows.reshape(value_rows.shape[0], KEY_VALUE_HEADS, HEAD_SIZE).transpose(1, 0, 2)


def merge_query(value_rows):
    return value_rows.transpose(1, 0, 2, 3).reshape(value_rows.shape[1], QUERY_HEADS * HEAD_SIZE)


def merge_keys(value_rows):
    return value_rows.transpose(1, 0, 2).reshape(value_rows.shape[1], KEY_VALUE_HEADS * HEAD_SIZE)


def attend(queries, keys_win, values_win, allowed):

    def one_head(parts):
        query_head, key_head, value_head = parts
        scores = (
            jnp.einsum("tgd,wd->gtw", query_head, key_head, preferred_element_type=jnp.float32)
            * SCORE_SCALE
        )
        scores = jnp.where(allowed[None], scores, -1e30)
        largest = jnp.max(scores, axis=-1, keepdims=True)
        expo_terms = jnp.exp(scores - largest)
        totals = jnp.sum(expo_terms, axis=-1, keepdims=True)
        probs_low = (expo_terms / totals).astype(jnp.bfloat16)
        mixed_head = jnp.einsum(
            "gtw,wd->tgd", probs_low, value_head, preferred_element_type=jnp.float32
        )
        return (mixed_head.astype(jnp.bfloat16), (largest + jnp.log(totals))[..., 0])

    heads_out, log_totals = lax.map(
        one_head, (split_query(queries), split_keys(keys_win), split_keys(values_win))
    )
    return (merge_query(heads_out), log_totals)


def attend_back(queries, keys_win, values_win, outputs, out_grads, log_totals, allowed):

    def one_head(parts):
        query_head, key_head, value_head, out_head, grad_head, lse_head = parts
        scores = (
            jnp.einsum("tgd,wd->gtw", query_head, key_head, preferred_element_type=jnp.float32)
            * SCORE_SCALE
        )
        scores = jnp.where(allowed[None], scores, -1e30)
        attn_probs = jnp.exp(scores - lse_head[..., None])
        probs_low = attn_probs.astype(jnp.bfloat16)
        value_part = jnp.einsum(
            "gtw,tgd->wd", probs_low, grad_head, preferred_element_type=jnp.float32
        )
        prob_part = jnp.einsum(
            "tgd,wd->gtw", grad_head, value_head, preferred_element_type=jnp.float32
        )
        delta_rows = jnp.sum(
            out_head.astype(jnp.float32) * grad_head.astype(jnp.float32), axis=-1
        ).T
        score_grad = (attn_probs * (prob_part - delta_rows[..., None]) * SCORE_SCALE).astype(
            jnp.bfloat16
        )
        query_part = jnp.einsum(
            "gtw,wd->tgd", score_grad, key_head, preferred_element_type=jnp.float32
        )
        key_part = jnp.einsum(
            "gtw,tgd->wd", score_grad, query_head, preferred_element_type=jnp.float32
        )
        return (query_part, key_part, value_part)

    parts = (
        split_query(queries),
        split_keys(keys_win),
        split_keys(values_win),
        split_query(outputs),
        split_query(out_grads),
        log_totals,
    )
    query_parts, key_parts, value_parts = lax.map(one_head, parts)
    return (merge_query(query_parts), merge_keys(key_parts), merge_keys(value_parts))


def local_gathered(
    inputs,
    lengths,
    routes,
    gain_attn,
    w_query,
    key_weight,
    value_weight,
    w_out,
    gain_ffn,
    w_router,
    w_gate,
    w_up,
    w_down,
    cotangent,
):
    layer_full = (
        lax.all_gather(gain_attn, ("expert", "shard"), axis=0, tiled=True),
        lax.all_gather(w_query, ("expert", "shard"), axis=0, tiled=True),
        lax.all_gather(key_weight, ("expert", "shard"), axis=0, tiled=True),
        lax.all_gather(value_weight, ("expert", "shard"), axis=0, tiled=True),
        lax.all_gather(w_out, ("expert", "shard"), axis=0, tiled=True),
        lax.all_gather(gain_ffn, ("expert", "shard"), axis=0, tiled=True),
        lax.all_gather(w_router, ("expert", "shard"), axis=0, tiled=True),
    )
    attn_gain_low, query_mat, key_matrix, value_mat, out_mat, ffn_gain_low, router_mat = layer_full
    gate_mat, up_mat, down_mat = (
        lax.all_gather(w_gate, "shard", axis=1, tiled=True),
        lax.all_gather(w_up, "shard", axis=1, tiled=True),
        lax.all_gather(w_down, "shard", axis=1, tiled=True),
    )
    attn_gain = attn_gain_low.astype(jnp.float32)
    ffn_gain = ffn_gain_low.astype(jnp.float32)
    row_count, model_width = inputs.shape
    owners = lax.axis_size("expert")
    place_id = lax.axis_index("shard")
    group_size = row_count * lax.axis_size("shard")
    longest = min(SEQ_MOST, group_size // 2)
    window_size = row_count + longest
    positions = place_id * row_count + jnp.arange(row_count, dtype=jnp.int32)
    seq_lengths = lengths[0]
    seq_ends = jnp.cumsum(seq_lengths)
    seq_starts = jnp.sum(
        jnp.where(seq_ends[None, :] <= positions[:, None], seq_lengths[None, :], 0), axis=1
    )
    sequence_offsets = positions - seq_starts
    key_pos = place_id * row_count - longest + jnp.arange(window_size, dtype=jnp.int32)
    allowed = (key_pos[None, :] >= seq_starts[:, None]) & (key_pos[None, :] <= positions[:, None])
    resid = inputs.astype(jnp.float32)
    normed_wide, inv_attn = norm_rows(resid, attn_gain)
    normalized_rows = normed_wide.astype(jnp.bfloat16)
    queries = apply_rotation(
        jnp.dot(normalized_rows, query_mat, preferred_element_type=jnp.float32),
        sequence_offsets,
        QUERY_HEADS,
        1.0,
    ).astype(jnp.bfloat16)
    keys_mine = apply_rotation(
        jnp.dot(normalized_rows, key_matrix, preferred_element_type=jnp.float32),
        sequence_offsets,
        KEY_VALUE_HEADS,
        1.0,
    ).astype(jnp.bfloat16)
    values_mine = jnp.dot(normalized_rows, value_mat, preferred_element_type=jnp.float32).astype(
        jnp.bfloat16
    )
    keys_group, values_group = (
        lax.all_gather(keys_mine, "shard", axis=0, tiled=True),
        lax.all_gather(values_mine, "shard", axis=0, tiled=True),
    )
    kv_width = keys_mine.shape[1]
    front_pad = jnp.zeros((longest, kv_width), jnp.bfloat16)
    keys_win = lax.dynamic_slice_in_dim(
        jnp.concatenate([front_pad, keys_group], axis=0), place_id * row_count, window_size, 0
    )
    values_win = lax.dynamic_slice_in_dim(
        jnp.concatenate([front_pad, values_group], axis=0), place_id * row_count, window_size, 0
    )
    attended, log_totals = attend(queries, keys_win, values_win, allowed)
    hidden = resid + jnp.dot(attended, out_mat, preferred_element_type=jnp.float32)
    normed2_wide, inv_ffn = norm_rows(hidden, ffn_gain)
    normed2 = normed2_wide.astype(jnp.bfloat16)
    expert_count = router_mat.shape[1]
    router_probs = jax.nn.softmax(
        jnp.dot(normed2, router_mat, preferred_element_type=jnp.float32), axis=-1
    )
    top_k = routes.shape[1]
    route_hits = (
        routes[:, :, None] == jnp.arange(expert_count, dtype=jnp.int32)[None, None, :]
    ).astype(jnp.float32)
    route_weights = jnp.sum(route_hits * router_probs[:, None, :], axis=-1)
    flat_routes = routes.reshape(-1)
    flat_hits = (flat_routes[:, None] == jnp.arange(expert_count, dtype=jnp.int32)[None, :]).astype(
        jnp.int32
    )
    slot_index = jnp.sum(flat_hits * (jnp.cumsum(flat_hits, axis=0) - 1), axis=1)
    dest_index = flat_routes * CAP + slot_index
    per_owner = expert_count // owners
    exp_local = gate_mat.shape[0]
    send_rows = (
        jnp.zeros((expert_count * CAP, model_width), jnp.bfloat16)
        .at[dest_index]
        .set(jnp.repeat(normed2, top_k, axis=0))
    )
    received = lax.all_to_all(
        send_rows.reshape(owners, per_owner * CAP, model_width),
        "expert",
        split_axis=0,
        concat_axis=0,
        tiled=True,
    )
    received = received.reshape(owners, exp_local, CAP, model_width)
    gate_pre = jnp.einsum("sjcd,jdf->sjcf", received, gate_mat, preferred_element_type=jnp.float32)
    up_pre = jnp.einsum("sjcd,jdf->sjcf", received, up_mat, preferred_element_type=jnp.float32)
    expert_act = (jax.nn.silu(gate_pre) * up_pre).astype(jnp.bfloat16)
    expert_rows = jnp.einsum(
        "sjcf,jfd->sjcd", expert_act, down_mat, preferred_element_type=jnp.float32
    ).astype(jnp.bfloat16)
    returned = lax.all_to_all(
        expert_rows.reshape(owners, per_owner * CAP, model_width),
        "expert",
        split_axis=0,
        concat_axis=0,
        tiled=True,
    )
    picked = (
        returned.reshape(expert_count * CAP, model_width)[dest_index]
        .reshape(row_count, top_k, model_width)
        .astype(jnp.float32)
    )
    output = (hidden + jnp.sum(route_weights[..., None] * picked, axis=1)).astype(jnp.bfloat16)
    upstream = cotangent.astype(jnp.float32)
    weight_grads = jnp.einsum("td,tkd->tk", upstream, picked)
    rows_grad = (
        (route_weights[..., None] * upstream[:, None, :])
        .astype(jnp.bfloat16)
        .reshape(row_count * top_k, model_width)
    )
    send_grads = (
        jnp.zeros((expert_count * CAP, model_width), jnp.bfloat16).at[dest_index].set(rows_grad)
    )
    recv_grads = lax.all_to_all(
        send_grads.reshape(owners, per_owner * CAP, model_width),
        "expert",
        split_axis=0,
        concat_axis=0,
        tiled=True,
    )
    recv_grads = recv_grads.reshape(owners, exp_local, CAP, model_width)
    act_grad = jnp.einsum(
        "sjcd,jfd->sjcf", recv_grads, down_mat, preferred_element_type=jnp.float32
    )
    sigma = jax.nn.sigmoid(gate_pre)
    gate_pre_grad = (act_grad * up_pre * sigma * (1.0 + gate_pre * (1.0 - sigma))).astype(
        jnp.bfloat16
    )
    up_pre_grad = (act_grad * gate_pre * sigma).astype(jnp.bfloat16)
    pair_grad = (
        jnp.einsum("sjcf,jdf->sjcd", gate_pre_grad, gate_mat, preferred_element_type=jnp.float32)
        + jnp.einsum("sjcf,jdf->sjcd", up_pre_grad, up_mat, preferred_element_type=jnp.float32)
    ).astype(jnp.bfloat16)
    pair_back = lax.all_to_all(
        pair_grad.reshape(owners, per_owner * CAP, model_width),
        "expert",
        split_axis=0,
        concat_axis=0,
        tiled=True,
    )
    normed2_grad = jnp.sum(
        pair_back.reshape(expert_count * CAP, model_width)[dest_index]
        .reshape(row_count, top_k, model_width)
        .astype(jnp.float32),
        axis=1,
    )
    down_part = jnp.einsum(
        "sjcf,sjcd->jfd", expert_act, recv_grads, preferred_element_type=jnp.float32
    )
    gate_part = jnp.einsum(
        "sjcd,sjcf->jdf", received, gate_pre_grad, preferred_element_type=jnp.float32
    )
    up_part = jnp.einsum(
        "sjcd,sjcf->jdf", received, up_pre_grad, preferred_element_type=jnp.float32
    )
    gate_share, up_share, down_final = (
        lax.psum_scatter(
            gate_part.astype(jnp.bfloat16), "shard", scatter_dimension=1, tiled=True
        ).astype(jnp.float32),
        lax.psum_scatter(
            up_part.astype(jnp.bfloat16), "shard", scatter_dimension=1, tiled=True
        ).astype(jnp.float32),
        lax.psum_scatter(
            down_part.astype(jnp.bfloat16), "shard", scatter_dimension=1, tiled=True
        ).astype(jnp.float32),
    )
    prob_grad = jnp.sum(route_hits * weight_grads[..., None], axis=1)
    logit_grad = (
        router_probs * (prob_grad - jnp.sum(router_probs * prob_grad, axis=-1, keepdims=True))
    ).astype(jnp.bfloat16)
    router_part = jnp.dot(normed2.T, logit_grad, preferred_element_type=jnp.float32)
    normed2_grad = normed2_grad + jnp.dot(
        logit_grad, router_mat.T, preferred_element_type=jnp.float32
    )
    gain_ffn_part, hidden_part = norm_back(normed2_grad, hidden, inv_ffn, ffn_gain)
    hidden_grad = upstream + hidden_part
    hidden_low = hidden_grad.astype(jnp.bfloat16)
    out_part = jnp.dot(attended.T, hidden_low, preferred_element_type=jnp.float32)
    attended_grad = jnp.dot(hidden_low, out_mat.T, preferred_element_type=jnp.float32).astype(
        jnp.bfloat16
    )
    query_raw, keys_part, values_part = attend_back(
        queries, keys_win, values_win, attended, attended_grad, log_totals, allowed
    )
    spread_zero = jnp.zeros((longest + group_size, kv_width), jnp.float32)
    keys_spread = lax.dynamic_update_slice_in_dim(spread_zero, keys_part, place_id * row_count, 0)[
        longest:
    ]
    values_spread = lax.dynamic_update_slice_in_dim(
        spread_zero, values_part, place_id * row_count, 0
    )[longest:]
    keys_unrotated, values_raw = (
        lax.psum_scatter(keys_spread, "shard", scatter_dimension=0, tiled=True),
        lax.psum_scatter(values_spread, "shard", scatter_dimension=0, tiled=True),
    )
    queries_grad = apply_rotation(query_raw, sequence_offsets, QUERY_HEADS, -1.0).astype(
        jnp.bfloat16
    )
    keys_gradient = apply_rotation(keys_unrotated, sequence_offsets, KEY_VALUE_HEADS, -1.0).astype(
        jnp.bfloat16
    )
    values_grad = values_raw.astype(jnp.bfloat16)
    query_part = jnp.dot(normalized_rows.T, queries_grad, preferred_element_type=jnp.float32)
    key_part = jnp.dot(normalized_rows.T, keys_gradient, preferred_element_type=jnp.float32)
    value_part = jnp.dot(normalized_rows.T, values_grad, preferred_element_type=jnp.float32)
    normed_grad = (
        jnp.dot(queries_grad, query_mat.T, preferred_element_type=jnp.float32)
        + jnp.dot(keys_gradient, key_matrix.T, preferred_element_type=jnp.float32)
        + jnp.dot(values_grad, value_mat.T, preferred_element_type=jnp.float32)
    )
    gain_attn_part, input_part = norm_back(normed_grad, resid, inv_attn, attn_gain)
    input_grad = hidden_grad + input_part
    layer_grads = (
        lax.psum_scatter(gain_attn_part, ("expert", "shard"), scatter_dimension=0, tiled=True),
        lax.psum_scatter(query_part, ("expert", "shard"), scatter_dimension=0, tiled=True),
        lax.psum_scatter(key_part, ("expert", "shard"), scatter_dimension=0, tiled=True),
        lax.psum_scatter(value_part, ("expert", "shard"), scatter_dimension=0, tiled=True),
        lax.psum_scatter(out_part, ("expert", "shard"), scatter_dimension=0, tiled=True),
        lax.psum_scatter(gain_ffn_part, ("expert", "shard"), scatter_dimension=0, tiled=True),
        lax.psum_scatter(router_part, ("expert", "shard"), scatter_dimension=0, tiled=True),
    )
    return (
        output,
        input_grad,
        layer_grads[0],
        layer_grads[1],
        layer_grads[2],
        layer_grads[3],
        layer_grads[4],
        layer_grads[5],
        layer_grads[6],
        gate_share,
        up_share,
        down_final,
    )


X_SWAP = [(i, i ^ 1) for i in range(4)]
Y_SWAP = [(i, i ^ 2) for i in range(4)]
PAD = 128


def core_swap(rows):
    count = lax.axis_size("shard")
    return lax.ppermute(rows, "shard", [(i, i ^ 1) for i in range(count)])


def chip_send(rows, step):
    count = lax.axis_size("shard")
    return lax.ppermute(rows, "shard", [(i, i ^ (2 * step)) for i in range(count)])


def x_send(rows):
    return lax.ppermute(rows, "expert", X_SWAP)


def y_send(rows):
    return lax.ppermute(rows, "expert", Y_SWAP)


def after(values, first):
    values, _ = lax.optimization_barrier((values, first))
    return values


def by_xor(blocks, index):
    blocks = jnp.where(index & 1, jnp.stack([blocks[1], blocks[0], blocks[3], blocks[2]]), blocks)
    return jnp.where(index & 2, jnp.stack([blocks[2], blocks[3], blocks[0], blocks[1]]), blocks)


def chips_gather(rows):
    return jnp.stack([rows] + [chip_send(rows, m) for m in range(1, 4)])


def plane_gather(block):
    half = block.shape[0] // 2
    from_x, from_y = x_send(block), y_send(block)
    far = jnp.concatenate([x_send(from_y[:half]), y_send(from_x[half:])])
    return jnp.stack([block, from_x, from_y, far])


def plane_reduce(blocks):
    half = blocks[0].shape[0] // 2
    low = jnp.bfloat16
    wide = jnp.float32
    far_x = x_send(blocks[3][:half])
    far_y = y_send(blocks[3][half:])
    for_x = jnp.concatenate(
        [blocks[1][:half], (blocks[1][half:].astype(wide) + far_y.astype(wide)).astype(low)]
    )
    for_y = jnp.concatenate(
        [(blocks[2][:half].astype(wide) + far_x.astype(wide)).astype(low), blocks[2][half:]]
    )
    from_x, from_y = x_send(for_x), y_send(for_y)
    return (blocks[0].astype(wide) + from_x.astype(wide) + from_y.astype(wide)).astype(low)


def chips_reduce(blocks):
    total = blocks[0].astype(jnp.float32)
    for m in range(1, 4):
        total = total + chip_send(blocks[m], m).astype(jnp.float32)
    return total


def attention(queries, keys, values, allowed):
    heads = queries.shape[1] // HEAD_SIZE
    query_heads = queries.reshape(-1, heads, HEAD_SIZE)
    scores = (
        jnp.einsum("tgd,wd->gtw", query_heads, keys, preferred_element_type=jnp.float32)
        * SCORE_SCALE
    )
    scores = jnp.where(allowed[None], scores, -1e30)
    largest = jnp.max(scores, axis=-1, keepdims=True)
    expo_terms = jnp.exp(scores - largest)
    totals = jnp.sum(expo_terms, axis=-1, keepdims=True)
    probs_low = (expo_terms / totals).astype(jnp.bfloat16)
    mixed = jnp.einsum("gtw,wd->tgd", probs_low, values, preferred_element_type=jnp.float32)
    return (mixed.astype(jnp.bfloat16).reshape(queries.shape), largest + jnp.log(totals))


def attention_back(queries, keys, values, outputs, out_grads, log_totals, allowed):
    heads = queries.shape[1] // HEAD_SIZE
    query_heads = queries.reshape(-1, heads, HEAD_SIZE)
    grad_heads = out_grads.reshape(-1, heads, HEAD_SIZE)
    out_heads = outputs.reshape(-1, heads, HEAD_SIZE)
    scores = (
        jnp.einsum("tgd,wd->gtw", query_heads, keys, preferred_element_type=jnp.float32)
        * SCORE_SCALE
    )
    scores = jnp.where(allowed[None], scores, -1e30)
    attn_probs = jnp.exp(scores - log_totals)
    probs_low = attn_probs.astype(jnp.bfloat16)
    value_part = jnp.einsum("gtw,tgd->wd", probs_low, grad_heads, preferred_element_type=jnp.float32)
    prob_part = jnp.einsum("tgd,wd->gtw", grad_heads, values, preferred_element_type=jnp.float32)
    delta_rows = jnp.sum(out_heads.astype(jnp.float32) * grad_heads.astype(jnp.float32), axis=-1).T
    score_grad = (attn_probs * (prob_part - delta_rows[..., None]) * SCORE_SCALE).astype(
        jnp.bfloat16
    )
    query_part = jnp.einsum("gtw,wd->tgd", score_grad, keys, preferred_element_type=jnp.float32)
    key_part = jnp.einsum("gtw,tgd->wd", score_grad, query_heads, preferred_element_type=jnp.float32)
    return (query_part.reshape(queries.shape), key_part, value_part)


def matmul(a, b, dims=((1,), (0,))):
    return lax.dot_general(a, b, (dims, ((), ())), preferred_element_type=jnp.float32)


def local_sliced(
    inputs,
    lengths,
    routes,
    gain_attn,
    w_query,
    key_weight,
    value_weight,
    w_out,
    gain_ffn,
    w_router,
    w_gate,
    w_up,
    w_down,
    cotangent,
):
    low = jnp.bfloat16
    wide = jnp.float32
    shards = lax.axis_size("shard")
    expert_id, shard_id = lax.axis_index("expert"), lax.axis_index("shard")
    chip_id, core_id = shard_id // 2, shard_id % 2
    row_count, model_width = inputs.shape
    group_size = row_count * shards
    weight_rows = w_query.shape[0]
    query_width = w_query.shape[1] // shards
    kv_width = key_weight.shape[1] // shards
    head_width = query_width + 2 * kv_width
    packed_width = head_width + kv_width
    expert_count = w_router.shape[1]
    per_owner, slice_rows, ff = w_gate.shape
    ff_slice = ff // shards
    unit_count = per_owner * ff_slice

    group_rows = lax.all_gather(inputs, "shard", axis=0, tiled=True)
    packed = jnp.concatenate(
        [
            w_query.reshape(weight_rows, shards, query_width),
            key_weight.reshape(weight_rows, shards, kv_width),
            value_weight.reshape(weight_rows, shards, kv_width),
            jnp.broadcast_to(gain_attn[:, None, None], (weight_rows, shards, kv_width)),
        ],
        axis=2,
    ).transpose(1, 0, 2)
    packed = lax.all_to_all(packed, "shard", 0, 0, tiled=True).reshape(-1, packed_width)
    head_weights = by_xor(plane_gather(packed), expert_id).reshape(model_width, packed_width)
    head_mat = head_weights[:, :head_width]
    attn_gain = head_weights[:, head_width].astype(wide)

    layer_pack = jnp.concatenate(
        [
            w_out,
            w_router,
            jnp.broadcast_to(gain_ffn[:, None], (weight_rows, PAD - expert_count)),
        ],
        axis=1,
    )
    layer_full = lax.all_gather(layer_pack, ("expert", "shard"), axis=0, tiled=True)
    out_mat = layer_full[:, :model_width]
    router_mat = layer_full[:, model_width : model_width + expert_count]
    ffn_gain = layer_full[:, model_width + expert_count].astype(wide)

    def columns_of(weight):
        pieces = weight.reshape(per_owner, slice_rows, shards, ff_slice).transpose(2, 1, 0, 3)
        pieces = pieces.reshape(shards, slice_rows, unit_count)
        mine = lax.all_to_all(pieces, "shard", 0, 0, tiled=True).reshape(model_width, unit_count)
        return jnp.concatenate([mine, core_swap(mine)], axis=1)

    gate_in, up_in, cot_in = after((w_gate, w_up, cotangent), group_rows)
    gate_mat, up_mat = columns_of(gate_in), columns_of(up_in)
    down_mine = w_down.reshape(unit_count, model_width)
    down_mat = jnp.concatenate([down_mine, core_swap(down_mine)], axis=0)

    up_rows = plane_gather(chips_gather(cot_in)).reshape(-1, model_width)

    positions = jnp.arange(group_size, dtype=jnp.int32)
    seq_lengths = lengths[0]
    seq_ends = jnp.cumsum(seq_lengths)
    seq_starts = jnp.sum(
        jnp.where(seq_ends[None, :] <= positions[:, None], seq_lengths[None, :], 0), axis=1
    )
    offsets = positions - seq_starts
    allowed = (positions[None, :] >= seq_starts[:, None]) & (
        positions[None, :] <= positions[:, None]
    )
    group_resid = group_rows.astype(wide)
    group_normed_wide, group_inv = norm_rows(group_resid, attn_gain)
    group_normed = group_normed_wide.astype(low)
    projected = matmul(group_normed, head_mat)
    queries = apply_rotation(
        projected[:, :query_width], offsets, query_width // HEAD_SIZE, 1.0
    ).astype(low)
    keys = apply_rotation(projected[:, query_width : query_width + kv_width], offsets, 1, 1.0)
    keys = keys.astype(low)
    values = projected[:, query_width + kv_width :].astype(low)
    head_attended, log_totals = attention(queries, keys, values, allowed)
    attended = lax.all_to_all(head_attended, "shard", 0, 1, tiled=True)

    resid = inputs.astype(wide)
    hidden = resid + matmul(attended, out_mat)
    normed2_wide, inv_ffn = norm_rows(hidden, ffn_gain)
    normed2 = normed2_wide.astype(low)
    router_probs = jax.nn.softmax(matmul(normed2, router_mat), axis=-1)
    route_hits = jnp.sum(
        (routes[:, :, None] == jnp.arange(expert_count, dtype=jnp.int32)).astype(wide), axis=1
    )
    route_weights = router_probs * route_hits
    weights_high = lax.reduce_precision(route_weights, 8, 7)
    weights_low = route_weights - weights_high
    sent_rows = jnp.concatenate(
        [
            normed2,
            weights_high.astype(low),
            weights_low.astype(low),
            jnp.zeros((row_count, PAD - 2 * expert_count), low),
        ],
        axis=1,
    )
    all_rows = plane_gather(chips_gather(sent_rows)).reshape(-1, model_width + PAD)
    expert_in = all_rows[:, :model_width]

    unit_expert = expert_id * per_owner + (jnp.arange(2 * unit_count) % unit_count) // ff_slice
    column = jnp.arange(PAD)[:, None]
    spread = ((column == unit_expert) | (column == unit_expert + expert_count)).astype(low)
    collect = (column == unit_expert).astype(low)
    pair_weight = matmul(all_rows[:, model_width:], spread)
    gate_pre = matmul(expert_in, gate_mat)
    up_pre = matmul(expert_in, up_mat)
    down_back = matmul(up_rows, down_mat, ((1,), (1,)))
    sigma = jax.nn.sigmoid(gate_pre)
    expert_act = gate_pre * sigma * up_pre
    act_weighted = (expert_act * pair_weight).astype(low)
    weight_terms = (expert_act * down_back).astype(low)
    act_grad = pair_weight * down_back
    gate_grad = (act_grad * up_pre * sigma * (1.0 + gate_pre * (1.0 - sigma))).astype(low)
    up_grad = (act_grad * gate_pre * sigma).astype(low)
    weight_cols = matmul(weight_terms, collect, ((1,), (1,)))
    rows_back = matmul(gate_grad, gate_mat, ((1,), (1,))) + matmul(up_grad, up_mat, ((1,), (1,)))
    back_sent = jnp.concatenate([rows_back.astype(low), weight_cols.astype(low)], axis=1)
    back_blocks = back_sent.reshape(4, 4, row_count, model_width + PAD)
    own_back = chips_reduce(plane_reduce(back_blocks))
    normed2_grad = own_back[:, :model_width]
    prob_grad = own_back[:, model_width : model_width + expert_count]

    mixed_part = matmul(act_weighted, down_mat).astype(low)
    mixed_part = after(mixed_part, own_back)
    mixed = chips_reduce(plane_reduce(mixed_part.reshape(4, 4, row_count, model_width)))
    output = (hidden + mixed).astype(low)

    def core_sum(part, axis):
        mine, theirs = jnp.split(part, 2, axis=axis)
        return mine + core_swap(theirs.astype(low)).astype(wide)

    def rows_of(part):
        total = core_sum(part, 1).astype(low).reshape(shards, slice_rows, unit_count)
        total = lax.all_to_all(total, "shard", 0, 0, tiled=True)
        total = total.reshape(shards, slice_rows, per_owner, ff_slice).transpose(2, 1, 0, 3)
        return total.reshape(per_owner, slice_rows, ff).astype(wide)

    gate_share = rows_of(matmul(expert_in, gate_grad, ((0,), (0,))))
    up_share = rows_of(matmul(expert_in, up_grad, ((0,), (0,))))
    down_final = core_sum(matmul(act_weighted, up_rows, ((0,), (0,))), 0)
    down_final = down_final.reshape(per_owner, ff_slice, model_width)

    upstream = cotangent.astype(wide)
    prob_grad = prob_grad * route_hits
    logit_grad = (
        router_probs * (prob_grad - jnp.sum(router_probs * prob_grad, axis=-1, keepdims=True))
    ).astype(low)
    router_part = matmul(normed2, logit_grad, ((0,), (0,)))
    normed2_grad = normed2_grad + matmul(logit_grad, router_mat, ((1,), (1,)))
    gain_ffn_part, hidden_part = norm_back(normed2_grad, hidden, inv_ffn, ffn_gain)
    hidden_grad = upstream + hidden_part
    hidden_low = hidden_grad.astype(low)
    attended_grad = matmul(hidden_low, out_mat, ((1,), (1,))).astype(low)
    head_attended_grad = lax.all_to_all(attended_grad, "shard", 1, 0, tiled=True)
    out_part = matmul(attended, hidden_low, ((0,), (0,)))
    layer_part = jnp.concatenate(
        [
            out_part,
            router_part,
            jnp.broadcast_to(gain_ffn_part[:, None], (model_width, PAD - expert_count)),
        ],
        axis=1,
    ).astype(low)
    layer_share = lax.psum_scatter(
        layer_part, ("expert", "shard"), scatter_dimension=0, tiled=True
    ).astype(wide)

    query_raw, keys_raw, values_raw = attention_back(
        queries, keys, values, head_attended, head_attended_grad, log_totals, allowed
    )
    queries_grad = apply_rotation(query_raw, offsets, query_width // HEAD_SIZE, -1.0)
    keys_grad = apply_rotation(keys_raw, offsets, 1, -1.0)
    projected_grad = jnp.concatenate([queries_grad, keys_grad, values_raw], axis=1).astype(low)
    normed_part = matmul(projected_grad, head_mat, ((1,), (1,)))
    gain_attn_part = jnp.sum(normed_part * group_resid * group_inv, axis=0)
    head_part = matmul(group_normed, projected_grad, ((0,), (0,)))

    blocks = normed_part.astype(low).reshape(shards // 2, 2, row_count, model_width)
    mine = jnp.where(core_id == 0, blocks[:, 0], blocks[:, 1])
    theirs = jnp.where(core_id == 0, blocks[:, 1], blocks[:, 0])
    summed = (mine.astype(wide) + core_swap(theirs).astype(wide)).astype(low)
    normed_grad = chips_reduce(by_xor(summed, chip_id))
    inv_attn = lax.rsqrt(jnp.mean(resid * resid, axis=-1, keepdims=True) + EPSILON)
    _, input_part = norm_back(normed_grad, resid, inv_attn, attn_gain)
    input_grad = hidden_grad + input_part

    head_pack = jnp.concatenate(
        [head_part, jnp.broadcast_to(gain_attn_part[:, None], (model_width, kv_width))], axis=1
    ).astype(low)
    head_blocks = by_xor(head_pack.reshape(4, model_width // 4, packed_width), expert_id)
    pair = head_blocks[:2].astype(wide) + y_send(head_blocks[2:]).astype(wide)
    head_share = pair[0] + x_send(pair[1].astype(low)).astype(wide)
    head_share = head_share.astype(low).reshape(shards, weight_rows, packed_width)
    head_share = lax.all_to_all(head_share, "shard", 0, 0, tiled=True).astype(wide)
    head_share = head_share.transpose(1, 0, 2)
    query_share = head_share[:, :, :query_width].reshape(weight_rows, -1)
    key_share = head_share[:, :, query_width : query_width + kv_width].reshape(weight_rows, -1)
    value_share = head_share[:, :, query_width + kv_width : head_width].reshape(weight_rows, -1)
    gain_attn_share = jnp.sum(head_share[:, :, head_width], axis=1)

    return (
        output,
        input_grad,
        gain_attn_share,
        query_share,
        key_share,
        value_share,
        layer_share[:, :model_width],
        layer_share[:, model_width + expert_count],
        layer_share[:, model_width : model_width + expert_count],
        gate_share,
        up_share,
        down_final,
    )


def solution(mesh):
    in_specs = (
        P(("expert", "shard"), None),
        P("expert", None),
        P(("expert", "shard"), None),
        P(("expert", "shard")),
        P(("expert", "shard"), None),
        P(("expert", "shard"), None),
        P(("expert", "shard"), None),
        P(("expert", "shard"), None),
        P(("expert", "shard")),
        P(("expert", "shard"), None),
        P("expert", "shard", None),
        P("expert", "shard", None),
        P("expert", "shard", None),
        P(("expert", "shard"), None),
    )
    out_specs = (
        P(("expert", "shard"), None),
        P(("expert", "shard"), None),
        P(("expert", "shard")),
        P(("expert", "shard"), None),
        P(("expert", "shard"), None),
        P(("expert", "shard"), None),
        P(("expert", "shard"), None),
        P(("expert", "shard")),
        P(("expert", "shard"), None),
        P("expert", "shard", None),
        P("expert", "shard", None),
        P("expert", "shard", None),
    )
    sliced = mesh.shape["shard"] == KEY_VALUE_HEADS and mesh.shape["expert"] == 4
    local = local_sliced if sliced else local_gathered
    return jax.shard_map(local, mesh=mesh, in_specs=in_specs, out_specs=out_specs, check_vma=False)
```

```python
import functools

import jax
import jax.numpy as jnp
from jax import lax
from jax.experimental import pallas as pl
from jax.experimental.pallas import tpu as pltpu
from jax.sharding import PartitionSpec as P

SHARD = "shard"
EXPERT = "expert"
QUERY_HEADS = 24
KEY_VALUE_HEADS = 8
HEAD_SIZE = 64
SEQ_MOST = 2048
CAP = 32


EPSILON = 1e-05
SCORE_SCALE = 0.125
ROPE_BASE = 10000.0


def apply_rotation(value_rows, positions, head_count, direction_sign):
    head_width = value_rows.shape[1] // head_count
    half_width = head_width // 2
    frequency = ROPE_BASE ** (-jnp.arange(half_width, dtype=jnp.float32) * 2.0 / head_width)
    angles = positions.astype(jnp.float32)[:, None] * frequency[None, :]
    cosine = jnp.cos(angles)[:, None, :]
    sine_part = direction_sign * jnp.sin(angles)[:, None, :]
    shaped = value_rows.reshape(value_rows.shape[0], head_count, head_width)
    first_half = shaped[..., :half_width]
    second_half = shaped[..., half_width:]
    turned = jnp.concatenate(
        [
            first_half * cosine - second_half * sine_part,
            second_half * cosine + first_half * sine_part,
        ],
        axis=-1,
    )
    return turned.reshape(value_rows.shape)


def norm_rows(value_rows, gain_row):
    inv_scale = lax.rsqrt(jnp.mean(value_rows * value_rows, axis=-1, keepdims=True) + EPSILON)
    return (value_rows * inv_scale * gain_row, inv_scale)


def norm_back(norm_grad, value_rows, inv_scale, gain_row):
    gain_part = jnp.sum(norm_grad * value_rows * inv_scale, axis=0)
    scaled = norm_grad * gain_row
    value_part = inv_scale * scaled - value_rows * inv_scale**3 * jnp.mean(
        scaled * value_rows, axis=-1, keepdims=True
    )
    return (gain_part, value_part)


def split_query(value_rows):
    return value_rows.reshape(
        value_rows.shape[0], KEY_VALUE_HEADS, QUERY_HEADS // KEY_VALUE_HEADS, HEAD_SIZE
    ).transpose(1, 0, 2, 3)


def split_keys(value_rows):
    return value_rows.reshape(value_rows.shape[0], KEY_VALUE_HEADS, HEAD_SIZE).transpose(1, 0, 2)


def merge_query(value_rows):
    return value_rows.transpose(1, 0, 2, 3).reshape(value_rows.shape[1], QUERY_HEADS * HEAD_SIZE)


def merge_keys(value_rows):
    return value_rows.transpose(1, 0, 2).reshape(value_rows.shape[1], KEY_VALUE_HEADS * HEAD_SIZE)


def attend(queries, keys_win, values_win, allowed):

    def one_head(parts):
        query_head, key_head, value_head = parts
        scores = (
            jnp.einsum("tgd,wd->gtw", query_head, key_head, preferred_element_type=jnp.float32)
            * SCORE_SCALE
        )
        scores = jnp.where(allowed[None], scores, -1e30)
        largest = jnp.max(scores, axis=-1, keepdims=True)
        expo_terms = jnp.exp(scores - largest)
        totals = jnp.sum(expo_terms, axis=-1, keepdims=True)
        probs_low = (expo_terms / totals).astype(jnp.bfloat16)
        mixed_head = jnp.einsum(
            "gtw,wd->tgd", probs_low, value_head, preferred_element_type=jnp.float32
        )
        return (mixed_head.astype(jnp.bfloat16), (largest + jnp.log(totals))[..., 0])

    heads_out, log_totals = lax.map(
        one_head, (split_query(queries), split_keys(keys_win), split_keys(values_win))
    )
    return (merge_query(heads_out), log_totals)


def attend_back(queries, keys_win, values_win, outputs, out_grads, log_totals, allowed):

    def one_head(parts):
        query_head, key_head, value_head, out_head, grad_head, lse_head = parts
        scores = (
            jnp.einsum("tgd,wd->gtw", query_head, key_head, preferred_element_type=jnp.float32)
            * SCORE_SCALE
        )
        scores = jnp.where(allowed[None], scores, -1e30)
        attn_probs = jnp.exp(scores - lse_head[..., None])
        probs_low = attn_probs.astype(jnp.bfloat16)
        value_part = jnp.einsum(
            "gtw,tgd->wd", probs_low, grad_head, preferred_element_type=jnp.float32
        )
        prob_part = jnp.einsum(
            "tgd,wd->gtw", grad_head, value_head, preferred_element_type=jnp.float32
        )
        delta_rows = jnp.sum(
            out_head.astype(jnp.float32) * grad_head.astype(jnp.float32), axis=-1
        ).T
        score_grad = (attn_probs * (prob_part - delta_rows[..., None]) * SCORE_SCALE).astype(
            jnp.bfloat16
        )
        query_part = jnp.einsum(
            "gtw,wd->tgd", score_grad, key_head, preferred_element_type=jnp.float32
        )
        key_part = jnp.einsum(
            "gtw,tgd->wd", score_grad, query_head, preferred_element_type=jnp.float32
        )
        return (query_part, key_part, value_part)

    parts = (
        split_query(queries),
        split_keys(keys_win),
        split_keys(values_win),
        split_query(outputs),
        split_query(out_grads),
        log_totals,
    )
    query_parts, key_parts, value_parts = lax.map(one_head, parts)
    return (merge_query(query_parts), merge_keys(key_parts), merge_keys(value_parts))


def local_gathered(
    inputs,
    lengths,
    routes,
    gain_attn,
    w_query,
    key_weight,
    value_weight,
    w_out,
    gain_ffn,
    w_router,
    w_gate,
    w_up,
    w_down,
    cotangent,
):
    layer_full = (
        lax.all_gather(gain_attn, (EXPERT, SHARD), axis=0, tiled=True),
        lax.all_gather(w_query, (EXPERT, SHARD), axis=0, tiled=True),
        lax.all_gather(key_weight, (EXPERT, SHARD), axis=0, tiled=True),
        lax.all_gather(value_weight, (EXPERT, SHARD), axis=0, tiled=True),
        lax.all_gather(w_out, (EXPERT, SHARD), axis=0, tiled=True),
        lax.all_gather(gain_ffn, (EXPERT, SHARD), axis=0, tiled=True),
        lax.all_gather(w_router, (EXPERT, SHARD), axis=0, tiled=True),
    )
    attn_gain_low, query_mat, key_matrix, value_mat, out_mat, ffn_gain_low, router_mat = layer_full
    gate_mat, up_mat, down_mat = (
        lax.all_gather(w_gate, SHARD, axis=1, tiled=True),
        lax.all_gather(w_up, SHARD, axis=1, tiled=True),
        lax.all_gather(w_down, SHARD, axis=1, tiled=True),
    )
    attn_gain = attn_gain_low.astype(jnp.float32)
    ffn_gain = ffn_gain_low.astype(jnp.float32)
    row_count, model_width = inputs.shape
    owners = lax.axis_size(EXPERT)
    place_id = lax.axis_index(SHARD)
    group_size = row_count * lax.axis_size(SHARD)
    longest = min(SEQ_MOST, group_size // 2)
    window_size = row_count + longest
    positions = place_id * row_count + jnp.arange(row_count, dtype=jnp.int32)
    seq_lengths = lengths[0]
    seq_ends = jnp.cumsum(seq_lengths)
    seq_starts = jnp.sum(
        jnp.where(seq_ends[None, :] <= positions[:, None], seq_lengths[None, :], 0), axis=1
    )
    sequence_offsets = positions - seq_starts
    key_pos = place_id * row_count - longest + jnp.arange(window_size, dtype=jnp.int32)
    allowed = (key_pos[None, :] >= seq_starts[:, None]) & (key_pos[None, :] <= positions[:, None])
    resid = inputs.astype(jnp.float32)
    normed_wide, inv_attn = norm_rows(resid, attn_gain)
    normalized_rows = normed_wide.astype(jnp.bfloat16)
    queries = apply_rotation(
        jnp.dot(normalized_rows, query_mat, preferred_element_type=jnp.float32),
        sequence_offsets,
        QUERY_HEADS,
        1.0,
    ).astype(jnp.bfloat16)
    keys_mine = apply_rotation(
        jnp.dot(normalized_rows, key_matrix, preferred_element_type=jnp.float32),
        sequence_offsets,
        KEY_VALUE_HEADS,
        1.0,
    ).astype(jnp.bfloat16)
    values_mine = jnp.dot(normalized_rows, value_mat, preferred_element_type=jnp.float32).astype(
        jnp.bfloat16
    )
    keys_group, values_group = (
        lax.all_gather(keys_mine, SHARD, axis=0, tiled=True),
        lax.all_gather(values_mine, SHARD, axis=0, tiled=True),
    )
    kv_width = keys_mine.shape[1]
    front_pad = jnp.zeros((longest, kv_width), jnp.bfloat16)
    keys_win = lax.dynamic_slice_in_dim(
        jnp.concatenate([front_pad, keys_group], axis=0), place_id * row_count, window_size, 0
    )
    values_win = lax.dynamic_slice_in_dim(
        jnp.concatenate([front_pad, values_group], axis=0), place_id * row_count, window_size, 0
    )
    attended, log_totals = attend(queries, keys_win, values_win, allowed)
    hidden = resid + jnp.dot(attended, out_mat, preferred_element_type=jnp.float32)
    normed2_wide, inv_ffn = norm_rows(hidden, ffn_gain)
    normed2 = normed2_wide.astype(jnp.bfloat16)
    expert_count = router_mat.shape[1]
    router_probs = jax.nn.softmax(
        jnp.dot(normed2, router_mat, preferred_element_type=jnp.float32), axis=-1
    )
    top_k = routes.shape[1]
    route_hits = (
        routes[:, :, None] == jnp.arange(expert_count, dtype=jnp.int32)[None, None, :]
    ).astype(jnp.float32)
    route_weights = jnp.sum(route_hits * router_probs[:, None, :], axis=-1)
    flat_routes = routes.reshape(-1)
    flat_hits = (flat_routes[:, None] == jnp.arange(expert_count, dtype=jnp.int32)[None, :]).astype(
        jnp.int32
    )
    slot_index = jnp.sum(flat_hits * (jnp.cumsum(flat_hits, axis=0) - 1), axis=1)
    dest_index = flat_routes * CAP + slot_index
    per_owner = expert_count // owners
    exp_local = gate_mat.shape[0]
    send_rows = (
        jnp.zeros((expert_count * CAP, model_width), jnp.bfloat16)
        .at[dest_index]
        .set(jnp.repeat(normed2, top_k, axis=0))
    )
    received = lax.all_to_all(
        send_rows.reshape(owners, per_owner * CAP, model_width),
        EXPERT,
        split_axis=0,
        concat_axis=0,
        tiled=True,
    )
    received = received.reshape(owners, exp_local, CAP, model_width)
    gate_pre = jnp.einsum("sjcd,jdf->sjcf", received, gate_mat, preferred_element_type=jnp.float32)
    up_pre = jnp.einsum("sjcd,jdf->sjcf", received, up_mat, preferred_element_type=jnp.float32)
    expert_act = (jax.nn.silu(gate_pre) * up_pre).astype(jnp.bfloat16)
    expert_rows = jnp.einsum(
        "sjcf,jfd->sjcd", expert_act, down_mat, preferred_element_type=jnp.float32
    ).astype(jnp.bfloat16)
    returned = lax.all_to_all(
        expert_rows.reshape(owners, per_owner * CAP, model_width),
        EXPERT,
        split_axis=0,
        concat_axis=0,
        tiled=True,
    )
    picked = (
        returned.reshape(expert_count * CAP, model_width)[dest_index]
        .reshape(row_count, top_k, model_width)
        .astype(jnp.float32)
    )
    output = (hidden + jnp.sum(route_weights[..., None] * picked, axis=1)).astype(jnp.bfloat16)
    upstream = cotangent.astype(jnp.float32)
    weight_grads = jnp.einsum("td,tkd->tk", upstream, picked)
    rows_grad = (
        (route_weights[..., None] * upstream[:, None, :])
        .astype(jnp.bfloat16)
        .reshape(row_count * top_k, model_width)
    )
    send_grads = (
        jnp.zeros((expert_count * CAP, model_width), jnp.bfloat16).at[dest_index].set(rows_grad)
    )
    recv_grads = lax.all_to_all(
        send_grads.reshape(owners, per_owner * CAP, model_width),
        EXPERT,
        split_axis=0,
        concat_axis=0,
        tiled=True,
    )
    recv_grads = recv_grads.reshape(owners, exp_local, CAP, model_width)
    act_grad = jnp.einsum(
        "sjcd,jfd->sjcf", recv_grads, down_mat, preferred_element_type=jnp.float32
    )
    sigma = jax.nn.sigmoid(gate_pre)
    gate_pre_grad = (act_grad * up_pre * sigma * (1.0 + gate_pre * (1.0 - sigma))).astype(
        jnp.bfloat16
    )
    up_pre_grad = (act_grad * gate_pre * sigma).astype(jnp.bfloat16)
    pair_grad = (
        jnp.einsum("sjcf,jdf->sjcd", gate_pre_grad, gate_mat, preferred_element_type=jnp.float32)
        + jnp.einsum("sjcf,jdf->sjcd", up_pre_grad, up_mat, preferred_element_type=jnp.float32)
    ).astype(jnp.bfloat16)
    pair_back = lax.all_to_all(
        pair_grad.reshape(owners, per_owner * CAP, model_width),
        EXPERT,
        split_axis=0,
        concat_axis=0,
        tiled=True,
    )
    normed2_grad = jnp.sum(
        pair_back.reshape(expert_count * CAP, model_width)[dest_index]
        .reshape(row_count, top_k, model_width)
        .astype(jnp.float32),
        axis=1,
    )
    down_part = jnp.einsum(
        "sjcf,sjcd->jfd", expert_act, recv_grads, preferred_element_type=jnp.float32
    )
    gate_part = jnp.einsum(
        "sjcd,sjcf->jdf", received, gate_pre_grad, preferred_element_type=jnp.float32
    )
    up_part = jnp.einsum(
        "sjcd,sjcf->jdf", received, up_pre_grad, preferred_element_type=jnp.float32
    )
    gate_share, up_share, down_final = (
        lax.psum_scatter(
            gate_part.astype(jnp.bfloat16), SHARD, scatter_dimension=1, tiled=True
        ).astype(jnp.float32),
        lax.psum_scatter(
            up_part.astype(jnp.bfloat16), SHARD, scatter_dimension=1, tiled=True
        ).astype(jnp.float32),
        lax.psum_scatter(
            down_part.astype(jnp.bfloat16), SHARD, scatter_dimension=1, tiled=True
        ).astype(jnp.float32),
    )
    prob_grad = jnp.sum(route_hits * weight_grads[..., None], axis=1)
    logit_grad = (
        router_probs * (prob_grad - jnp.sum(router_probs * prob_grad, axis=-1, keepdims=True))
    ).astype(jnp.bfloat16)
    router_part = jnp.dot(normed2.T, logit_grad, preferred_element_type=jnp.float32)
    normed2_grad = normed2_grad + jnp.dot(
        logit_grad, router_mat.T, preferred_element_type=jnp.float32
    )
    gain_ffn_part, hidden_part = norm_back(normed2_grad, hidden, inv_ffn, ffn_gain)
    hidden_grad = upstream + hidden_part
    hidden_low = hidden_grad.astype(jnp.bfloat16)
    out_part = jnp.dot(attended.T, hidden_low, preferred_element_type=jnp.float32)
    attended_grad = jnp.dot(hidden_low, out_mat.T, preferred_element_type=jnp.float32).astype(
        jnp.bfloat16
    )
    query_raw, keys_part, values_part = attend_back(
        queries, keys_win, values_win, attended, attended_grad, log_totals, allowed
    )
    spread_zero = jnp.zeros((longest + group_size, kv_width), jnp.float32)
    keys_spread = lax.dynamic_update_slice_in_dim(spread_zero, keys_part, place_id * row_count, 0)[
        longest:
    ]
    values_spread = lax.dynamic_update_slice_in_dim(
        spread_zero, values_part, place_id * row_count, 0
    )[longest:]
    keys_unrotated, values_raw = (
        lax.psum_scatter(keys_spread, SHARD, scatter_dimension=0, tiled=True),
        lax.psum_scatter(values_spread, SHARD, scatter_dimension=0, tiled=True),
    )
    queries_grad = apply_rotation(query_raw, sequence_offsets, QUERY_HEADS, -1.0).astype(
        jnp.bfloat16
    )
    keys_gradient = apply_rotation(keys_unrotated, sequence_offsets, KEY_VALUE_HEADS, -1.0).astype(
        jnp.bfloat16
    )
    values_grad = values_raw.astype(jnp.bfloat16)
    query_part = jnp.dot(normalized_rows.T, queries_grad, preferred_element_type=jnp.float32)
    key_part = jnp.dot(normalized_rows.T, keys_gradient, preferred_element_type=jnp.float32)
    value_part = jnp.dot(normalized_rows.T, values_grad, preferred_element_type=jnp.float32)
    normed_grad = (
        jnp.dot(queries_grad, query_mat.T, preferred_element_type=jnp.float32)
        + jnp.dot(keys_gradient, key_matrix.T, preferred_element_type=jnp.float32)
        + jnp.dot(values_grad, value_mat.T, preferred_element_type=jnp.float32)
    )
    gain_attn_part, input_part = norm_back(normed_grad, resid, inv_attn, attn_gain)
    input_grad = hidden_grad + input_part
    layer_grads = (
        lax.psum_scatter(gain_attn_part, (EXPERT, SHARD), scatter_dimension=0, tiled=True),
        lax.psum_scatter(query_part, (EXPERT, SHARD), scatter_dimension=0, tiled=True),
        lax.psum_scatter(key_part, (EXPERT, SHARD), scatter_dimension=0, tiled=True),
        lax.psum_scatter(value_part, (EXPERT, SHARD), scatter_dimension=0, tiled=True),
        lax.psum_scatter(out_part, (EXPERT, SHARD), scatter_dimension=0, tiled=True),
        lax.psum_scatter(gain_ffn_part, (EXPERT, SHARD), scatter_dimension=0, tiled=True),
        lax.psum_scatter(router_part, (EXPERT, SHARD), scatter_dimension=0, tiled=True),
    )
    return (
        output,
        input_grad,
        layer_grads[0],
        layer_grads[1],
        layer_grads[2],
        layer_grads[3],
        layer_grads[4],
        layer_grads[5],
        layer_grads[6],
        gate_share,
        up_share,
        down_final,
    )


VMEM_MOST = 60 * 1024 * 1024
ROW_TILE = 256
QUERY_TILE = 256
PAD = 128


def mm(a, b):
    return jnp.dot(a, b, preferred_element_type=jnp.float32)


def mm_t(a, b):
    return lax.dot_general(a, b, (((1,), (1,)), ((), ())), preferred_element_type=jnp.float32)


def t_mm(a, b):
    return lax.dot_general(a, b, (((0,), (0,)), ((), ())), preferred_element_type=jnp.float32)


def lane_row(rows, lane):
    lanes = lax.broadcasted_iota(jnp.int32, (8, rows.shape[1]), 1)
    return mm_t((lanes == lane).astype(rows.dtype), rows)[:1]


def tile_spec(rows, cols):
    return pl.BlockSpec((rows, cols), lambda i, *_: (i, 0))


def whole_spec(array):
    zeros = (0,) * len(array.shape)
    return pl.BlockSpec(array.shape, lambda *_: zeros, pipeline_mode=pl.Buffered(1))


def turn(rows, cosine, sine):
    lane = lax.broadcasted_iota(jnp.int32, rows.shape, 1)
    width = rows.shape[1]
    half = HEAD_SIZE // 2
    other = jnp.where(
        lane % HEAD_SIZE < half, pltpu.roll(rows, width - half, 1), pltpu.roll(rows, half, 1)
    )
    return rows * cosine + other * sine


def stacked(rows, heads):
    return jnp.concatenate(
        [rows[:, h * HEAD_SIZE : (h + 1) * HEAD_SIZE] for h in range(heads)], axis=0
    )


def side_by_side(rows, heads):
    count = rows.shape[0] // heads
    return jnp.concatenate([rows[h * count : (h + 1) * count] for h in range(heads)], axis=1)


def head_lanes(ref, heads):
    return jnp.concatenate(
        [
            ref[d, h * HEAD_SIZE : (h + 1) * HEAD_SIZE, :]
            for h in range(heads)
            for d in range(ref.shape[0])
        ],
        axis=1,
    )


def scores_of(keys, queries, start_row, step):
    scores = mm_t(keys, queries) * SCORE_SCALE
    key_pos = lax.broadcasted_iota(jnp.int32, scores.shape, 0)
    lane = lax.broadcasted_iota(jnp.int32, (1, scores.shape[1]), 1)
    query_pos = step * QUERY_TILE + lane % QUERY_TILE
    allowed = (key_pos >= start_row) & (key_pos <= query_pos)
    return jnp.where(allowed, scores, -1e30)


def tiles_of(ref):
    return ref.shape[0] // QUERY_TILE


def attend_kernel(
    heads,
    places,
    own_ref,
    other_ref,
    mat_ref,
    cos_ref,
    sin_ref,
    start_ref,
    unit_ref,
    normed_ref,
    qkv_ref,
    out_ref,
    lse_ref,
    keys_all,
    values_all,
    gain_row,
):
    step = pl.program_id(0)
    low, wide = jnp.bfloat16, jnp.float32
    query_width = heads * HEAD_SIZE
    turned_width = query_width + HEAD_SIZE

    @pl.when(step == 0)
    def _():
        keys_all[...] = jnp.zeros_like(keys_all)
        values_all[...] = jnp.zeros_like(values_all)
        gain_row[...] = lane_row(mat_ref[:, turned_width:], HEAD_SIZE)

    own, other = own_ref[0].astype(wide), other_ref[0].astype(wide)
    first = places[tiles_of(keys_all)] == 0
    x = jnp.concatenate([jnp.where(first, own, other), jnp.where(first, other, own)], axis=0)
    scaled = x * lax.rsqrt(jnp.mean(x * x, axis=-1, keepdims=True) + EPSILON)
    unit_ref[...] = scaled.astype(low)
    normed = (scaled * gain_row[...]).astype(low)
    normed_ref[...] = normed
    projected = mm(normed, mat_ref[...])
    turned = turn(projected[:, :turned_width], cos_ref[...], sin_ref[...]).astype(low)
    values = projected[:, turned_width:].astype(low)
    qkv_ref[:, :turned_width] = turned
    qkv_ref[:, turned_width:] = values
    here = pl.ds(pl.multiple_of(step * QUERY_TILE, QUERY_TILE), QUERY_TILE)
    keys_all[here, :] = turned[:, query_width:]
    values_all[here, :] = values[:, :HEAD_SIZE]
    queries = stacked(turned[:, :query_width], heads)
    scores = scores_of(keys_all[...], queries, start_ref[0], step)
    largest = jnp.max(scores, axis=0, keepdims=True)
    terms = jnp.exp(scores - largest)
    totals = jnp.sum(terms, axis=0, keepdims=True)
    probs = (terms / totals).astype(low)
    mixed = t_mm(values_all[...], probs).astype(low)
    blocks, _, block_rows = out_ref.shape
    for h in range(heads):
        for d in range(blocks):
            first_lane = h * QUERY_TILE + d * block_rows
            out_ref[d, h * HEAD_SIZE : (h + 1) * HEAD_SIZE, :] = mixed[
                :, first_lane : first_lane + block_rows
            ]
    lse_ref[0] = largest + jnp.log(totals)


def attend_rows(places, own_rows, other_rows, mat, cosine, sine, starts):
    low = jnp.bfloat16
    tiles, part, width = own_rows.shape
    rows = tiles * QUERY_TILE
    packed = mat.shape[1]
    heads = packed // HEAD_SIZE - 3
    lanes = pl.BlockSpec((1, 1, heads * QUERY_TILE), lambda i, _: (i, 0, 0))
    turned_width = (heads + 1) * HEAD_SIZE
    return pl.pallas_call(
        functools.partial(attend_kernel, heads),
        grid_spec=pltpu.PrefetchScalarGridSpec(
            num_scalar_prefetch=1,
            grid=(tiles,),
            in_specs=[
                pl.BlockSpec((1, part, width), lambda i, at: (at[i], 0, 0)),
                pl.BlockSpec((1, part, width), lambda i, at: (at[i], 0, 0)),
                whole_spec(mat),
                tile_spec(QUERY_TILE, turned_width),
                tile_spec(QUERY_TILE, turned_width),
                lanes,
            ],
            out_specs=[
                tile_spec(QUERY_TILE, width),
                tile_spec(QUERY_TILE, width),
                tile_spec(QUERY_TILE, packed),
                pl.BlockSpec((QUERY_TILE // part, heads * HEAD_SIZE, part), lambda i, _: (i, 0, 0)),
                lanes,
            ],
            scratch_shapes=[
                pltpu.VMEM((rows, HEAD_SIZE), low),
                pltpu.VMEM((rows, HEAD_SIZE), low),
                pltpu.VMEM((1, width), jnp.float32),
            ],
        ),
        out_shape=[
            jax.ShapeDtypeStruct((rows, width), low),
            jax.ShapeDtypeStruct((rows, width), low),
            jax.ShapeDtypeStruct((rows, packed), low),
            jax.ShapeDtypeStruct((rows // part, heads * HEAD_SIZE, part), low),
            jax.ShapeDtypeStruct((tiles, 1, heads * QUERY_TILE), jnp.float32),
        ],
        compiler_params=pltpu.CompilerParams(vmem_limit_bytes=VMEM_MOST),
        cost_estimate=pl.CostEstimate(
            flops=9_000_000_000, bytes_accessed=20_000_000, transcendentals=3_000_000
        ),
    )(places, own_rows, other_rows, mat, cosine, sine, starts)


def attend_back_kernel(
    heads,
    qkv_ref,
    out_ref,
    grad_ref,
    lse_ref,
    cos_ref,
    sin_ref,
    start_ref,
    grads_ref,
    keys_acc,
    values_acc,
    queries_grad,
):
    step = pl.program_id(0)
    low, wide = jnp.bfloat16, jnp.float32
    query_width = heads * HEAD_SIZE
    turned_width = query_width + HEAD_SIZE

    @pl.when(step == 0)
    def _():
        keys_acc[...] = jnp.zeros_like(keys_acc)
        values_acc[...] = jnp.zeros_like(values_acc)

    here = pl.ds(pl.multiple_of(step * QUERY_TILE, QUERY_TILE), QUERY_TILE)
    keys = qkv_ref[:, query_width:turned_width]
    values = qkv_ref[:, turned_width : turned_width + HEAD_SIZE]
    queries = stacked(qkv_ref[here, :query_width], heads)
    grads = head_lanes(grad_ref, heads)
    outs = head_lanes(out_ref, heads)
    delta = jnp.sum(outs.astype(wide) * grads.astype(wide), axis=0, keepdims=True)
    scores = scores_of(keys, queries, start_ref[0], step)
    probs = jnp.exp(scores - lse_ref[0])
    values_acc[...] += mm_t(probs.astype(low), grads)
    score_grad = (probs * (mm(values, grads) - delta) * SCORE_SCALE).astype(low)
    keys_acc[...] += mm(score_grad, queries)
    queries_grad[here, :] = side_by_side(t_mm(keys, score_grad).T, heads)

    @pl.when(step == pl.num_programs(0) - 1)
    def _():
        both = jnp.concatenate([queries_grad[...], keys_acc[...]], axis=1)
        grads_ref[:, :turned_width] = turn(both, cos_ref[...], -sin_ref[...]).astype(low)
        grads_ref[:, turned_width:] = jnp.concatenate(
            [values_acc[...].astype(low), jnp.zeros(values_acc.shape, low)], axis=1
        )


def attend_rows_back(qkv, out, grad, lse, cosine, sine, starts):
    rows, packed = qkv.shape
    heads = packed // HEAD_SIZE - 3
    tiles = rows // QUERY_TILE
    lanes = pl.BlockSpec((1, 1, heads * QUERY_TILE), lambda i: (i, 0, 0))
    part = out.shape[2]
    blocks = pl.BlockSpec((QUERY_TILE // part, heads * HEAD_SIZE, part), lambda i: (i, 0, 0))
    return pl.pallas_call(
        functools.partial(attend_back_kernel, heads),
        grid=(tiles,),
        in_specs=[
            whole_spec(qkv),
            blocks,
            blocks,
            lanes,
            whole_spec(cosine),
            whole_spec(sine),
            lanes,
        ],
        out_specs=pl.BlockSpec((rows, packed), lambda i: (0, 0)),
        out_shape=jax.ShapeDtypeStruct((rows, packed), jnp.bfloat16),
        scratch_shapes=[
            pltpu.VMEM((rows, HEAD_SIZE), jnp.float32),
            pltpu.VMEM((rows, HEAD_SIZE), jnp.float32),
            pltpu.VMEM((rows, heads * HEAD_SIZE), jnp.float32),
        ],
        compiler_params=pltpu.CompilerParams(vmem_limit_bytes=VMEM_MOST),
        cost_estimate=pl.CostEstimate(
            flops=10_000_000_000, bytes_accessed=20_000_000, transcendentals=3_000_000
        ),
    )(qkv, out, grad, lse, cosine, sine, starts)


def own_forward_kernel(
    expert_count, attended_ref, layer_ref, x_ref, hits_ref, hidden_ref, sent_ref, probs_ref
):
    low, wide = jnp.bfloat16, jnp.float32
    width = x_ref.shape[1]
    attended = attended_ref[...].reshape(width, attended_ref.shape[2])
    hidden = x_ref[...].astype(wide) + t_mm(attended, layer_ref[:, :width])
    hidden_ref[...] = hidden
    inv = lax.rsqrt(jnp.mean(hidden * hidden, axis=-1, keepdims=True) + EPSILON)
    normed = (hidden * inv * lane_row(layer_ref[:, width:], expert_count)).astype(low)
    sent_ref[:, :width] = normed
    logits = mm(normed, layer_ref[:, width:])
    lane = lax.broadcasted_iota(jnp.int32, logits.shape, 1)
    logits = jnp.where(lane < expert_count, logits, -1e30)
    terms = jnp.exp(logits - jnp.max(logits, axis=-1, keepdims=True))
    probs = terms / jnp.sum(terms, axis=-1, keepdims=True)
    probs_ref[...] = probs
    weights = probs * hits_ref[...]
    high = weights.astype(low).astype(wide)
    rest = pltpu.roll(weights - high, expert_count, 1)
    sent_ref[:, width:] = (high + rest).astype(low)


def own_forward(attended, layer_full, x, hits, expert_count):
    rows, width = x.shape
    return pl.pallas_call(
        functools.partial(own_forward_kernel, expert_count),
        out_shape=[
            jax.ShapeDtypeStruct((rows, width), jnp.float32),
            jax.ShapeDtypeStruct((rows, width + PAD), jnp.bfloat16),
            jax.ShapeDtypeStruct((rows, PAD), jnp.float32),
        ],
        compiler_params=pltpu.CompilerParams(vmem_limit_bytes=VMEM_MOST),
        cost_estimate=pl.CostEstimate(
            flops=3_000_000_000, bytes_accessed=10_000_000, transcendentals=20_000
        ),
    )(attended, layer_full, x, hits)


def own_backward_kernel(
    expert_count,
    back0_ref,
    back1_ref,
    back2_ref,
    back3_ref,
    probs_ref,
    hits_ref,
    hidden_ref,
    layer_ref,
    up_ref,
    grad_ref,
    attended_grad_ref,
    logit_ref,
    gain_ref,
):
    low, wide = jnp.bfloat16, jnp.float32
    width = up_ref.shape[1]
    total = back0_ref[...].astype(wide) + back1_ref[...].astype(wide)
    total += back2_ref[...].astype(wide) + back3_ref[...].astype(wide)
    probs = probs_ref[...]
    prob_grad = total[:, width:] * hits_ref[...]
    logit_grad = probs * (prob_grad - jnp.sum(probs * prob_grad, axis=-1, keepdims=True))
    logit_low = logit_grad.astype(low)
    logit_ref[...] = logit_low
    normed_grad = total[:, :width] + mm_t(logit_low, layer_ref[:, width:])
    hidden = hidden_ref[...]
    inv = lax.rsqrt(jnp.mean(hidden * hidden, axis=-1, keepdims=True) + EPSILON)
    gain_ref[...] = (normed_grad * hidden * inv).astype(low)
    scaled = normed_grad * lane_row(layer_ref[:, width:], expert_count)
    hidden_part = inv * scaled - hidden * inv * inv * inv * jnp.mean(
        scaled * hidden, axis=-1, keepdims=True
    )
    hidden_grad = up_ref[...].astype(wide) + hidden_part
    grad_ref[...] = hidden_grad
    attended_grad = mm_t(layer_ref[:, :width], hidden_grad.astype(low)).astype(low)
    attended_grad_ref[...] = attended_grad.reshape(attended_grad_ref.shape)


def own_backward(backs, probs, hits, hidden, layer_full, cotangent, heads_shape, expert_count):
    rows, width = cotangent.shape
    low = jnp.bfloat16
    return pl.pallas_call(
        functools.partial(own_backward_kernel, expert_count),
        out_shape=[
            jax.ShapeDtypeStruct((rows, width), jnp.float32),
            jax.ShapeDtypeStruct(heads_shape, low),
            jax.ShapeDtypeStruct((rows, PAD), low),
            jax.ShapeDtypeStruct((rows, width), low),
        ],
        compiler_params=pltpu.CompilerParams(vmem_limit_bytes=VMEM_MOST),
        cost_estimate=pl.CostEstimate(
            flops=3_000_000_000, bytes_accessed=10_000_000, transcendentals=1_000
        ),
    )(*backs, probs, hits, hidden, layer_full, cotangent)


def layer_grads_kernel(
    expert_count, attended_ref, grad_ref, sent_ref, logit_ref, gain_ref, out_ref
):
    low = jnp.bfloat16
    width = grad_ref.shape[1]
    attended = attended_ref[...].reshape(width, attended_ref.shape[2])
    out_ref[:, :width] = mm(attended, grad_ref[...].astype(low)).astype(low)
    lane = lax.broadcasted_iota(jnp.int32, logit_ref.shape, 1)
    ones = (lane == expert_count).astype(low)
    tail = t_mm(sent_ref[:, :width], logit_ref[...]) + t_mm(gain_ref[...], ones)
    out_ref[:, width:] = tail.astype(low)


def layer_grads(attended, hidden_grad, sent_rows, logit_grad, gain_terms, expert_count):
    width = hidden_grad.shape[1]
    return pl.pallas_call(
        functools.partial(layer_grads_kernel, expert_count),
        out_shape=jax.ShapeDtypeStruct((width, width + PAD), jnp.bfloat16),
        compiler_params=pltpu.CompilerParams(vmem_limit_bytes=VMEM_MOST),
        cost_estimate=pl.CostEstimate(
            flops=3_000_000_000, bytes_accessed=8_000_000, transcendentals=0
        ),
    )(attended, hidden_grad, sent_rows, logit_grad, gain_terms)


def tile_parts(pieces):
    half = ROW_TILE // 2
    parts = [p.at[i * half : (i + 1) * half] for p in pieces for i in range(p.shape[0] // half)]
    return [parts[i : i + 2] for i in range(0, len(parts), 2)]


def expert_kernel(counts, *refs):
    places, refs = refs[0], refs[1:]

    def take(count):
        nonlocal refs
        taken, refs = refs[:count], refs[count:]
        return taken

    row_refs, up_refs = take(counts), take(counts)
    weight_refs, down_refs, (spread_ref,) = take(8), take(2), take(1)
    back_refs, mix_refs = take(counts), take(counts)
    rows_out, ups_out, act_ref, gate_grad_ref, up_grad_ref = take(5)
    gate_mat, up_mat, down_mat, rows, ups, backs, mixes = take(7)
    back_acc, mix_acc, cols_acc, weight_sems, in_sems, out_sems = refs
    low = jnp.bfloat16
    step, steps = pl.program_id(0), pl.num_programs(0)
    slot = lax.rem(step, 2)
    experts_here, width, unit = gate_mat.shape
    slice_rows = weight_refs[0].shape[2]
    half = ROW_TILE // 2
    halves = (slice(0, half), slice(half, ROW_TILE))
    sources = list(zip(tile_parts(row_refs), tile_parts(up_refs)))
    targets = list(zip(tile_parts(back_refs), tile_parts(mix_refs)))

    def weight_copies():
        for p, piece in enumerate(weight_refs):
            at = pl.ds(pl.multiple_of(places[p] * slice_rows, slice_rows), slice_rows)
            for t, mat in enumerate((gate_mat, up_mat)):
                yield pltpu.make_async_copy(
                    piece.at[t], mat.at[:, at, :], weight_sems.at[2 * p + t]
                )
        share = down_refs[0].shape[1]
        for p, piece in enumerate(down_refs):
            at = pl.ds(pl.multiple_of(places[8 + p] * share, share), share)
            yield pltpu.make_async_copy(piece, down_mat.at[:, at, :], weight_sems.at[16 + p])

    def tile_in(tile, at):
        for h in range(2):
            for i, (parts, held) in enumerate(zip(sources[tile], (rows, ups))):
                yield pltpu.make_async_copy(
                    parts[h], held.at[at, halves[h]], in_sems.at[at, 2 * h + i]
                )

    def tile_out(tile, at):
        for h in range(2):
            for i, (parts, held) in enumerate(zip(targets[tile], (backs, mixes))):
                yield pltpu.make_async_copy(
                    held.at[at, halves[h]], parts[h], out_sems.at[at, 2 * h + i]
                )

    @pl.when(step == 0)
    def _():
        for copy in tile_in(0, 0):
            copy.start()
        for copy in weight_copies():
            copy.start()

    for tile in range(1, len(sources)):

        @pl.when(step + 1 == tile)
        def _():
            for copy in tile_in(tile, tile % 2):
                copy.start()

    for copy in tile_in(0, slot):
        copy.wait()

    @pl.when(step == 0)
    def _():
        for copy in weight_copies():
            copy.wait()

    x = rows[slot, :, :width]
    weights = rows[slot, :, width:]
    u = ups[slot]
    rows_out[...] = x
    ups_out[...] = u
    pair = 2
    for c in range(experts_here // pair):
        at = slice(c * pair * unit, (c + 1) * pair * unit)
        both = slice(c * pair, (c + 1) * pair)
        gate_here = jnp.concatenate([gate_mat[c * pair + i] for i in range(pair)], axis=1)
        up_here = jnp.concatenate([up_mat[c * pair + i] for i in range(pair)], axis=1)
        down_here = down_mat[both].reshape(pair * unit, width)
        gate_pre = mm(x, gate_here)
        up_pre = mm(x, up_here)
        down_back = mm_t(u, down_here)
        pair_weight = mm(weights, spread_ref[:, at])
        sigma = jax.nn.sigmoid(gate_pre)
        gated = gate_pre * sigma
        act = gated * up_pre
        act_low = (act * pair_weight).astype(low)
        terms = (act * down_back).astype(low)
        act_grad = pair_weight * down_back
        gate_low = (act_grad * up_pre * (sigma + gated * (1.0 - sigma))).astype(low)
        up_low = (act_grad * gated).astype(low)
        act_ref[:, at] = act_low
        gate_grad_ref[:, at] = gate_low
        up_grad_ref[:, at] = up_low
        back = mm_t(gate_low, gate_here) + mm_t(up_low, up_here)
        mixed = mm(act_low, down_here)
        cols = mm_t(terms, spread_ref[:, at])
        if c == 0:
            back_acc[...] = back
            mix_acc[...] = mixed
            cols_acc[...] = cols
        else:
            back_acc[...] += back
            mix_acc[...] += mixed
            cols_acc[...] += cols

    @pl.when(step >= 2)
    def _():
        for copy in tile_out(0, slot):
            copy.wait()

    backs[slot, :, :width] = back_acc[...].astype(low)
    backs[slot, :, width:] = cols_acc[...].astype(low)
    mixes[slot] = mix_acc[...].astype(low)
    for tile in range(len(targets)):

        @pl.when(step == tile)
        def _():
            for copy in tile_out(tile, tile % 2):
                copy.start()

    @pl.when(step == steps - 1)
    def _():
        for copy in tile_out(0, 1 - slot):
            copy.wait()
        for copy in tile_out(0, slot):
            copy.wait()


def experts(places, row_pieces, up_pieces, weight_pieces, down_pieces, spread):
    low, wide = jnp.bfloat16, jnp.float32
    width = up_pieces[0].shape[1]
    padded = row_pieces[0].shape[1]
    experts_here = down_pieces[0].shape[0]
    units = spread.shape[1]
    unit = units // experts_here
    total = sum(p.shape[0] for p in row_pieces)
    counts = len(row_pieces)
    anywhere = pl.BlockSpec(memory_space=pl.ANY)
    out = pl.pallas_call(
        functools.partial(expert_kernel, counts),
        grid_spec=pltpu.PrefetchScalarGridSpec(
            num_scalar_prefetch=1,
            grid=(total // ROW_TILE,),
            in_specs=[anywhere] * (2 * counts + 10) + [whole_spec(spread)],
            out_specs=[anywhere] * (2 * counts)
            + [tile_spec(ROW_TILE, width)] * 2
            + [tile_spec(ROW_TILE, units)] * 3,
            scratch_shapes=[
                pltpu.VMEM((experts_here, width, unit), low),
                pltpu.VMEM((experts_here, width, unit), low),
                pltpu.VMEM((experts_here, unit, width), low),
                pltpu.VMEM((2, ROW_TILE, padded), low),
                pltpu.VMEM((2, ROW_TILE, width), low),
                pltpu.VMEM((2, ROW_TILE, padded), low),
                pltpu.VMEM((2, ROW_TILE, width), low),
                pltpu.VMEM((ROW_TILE, width), wide),
                pltpu.VMEM((ROW_TILE, width), wide),
                pltpu.VMEM((ROW_TILE, padded - width), wide),
                pltpu.SemaphoreType.DMA((18,)),
                pltpu.SemaphoreType.DMA((2, 4)),
                pltpu.SemaphoreType.DMA((2, 4)),
            ],
        ),
        out_shape=[jax.ShapeDtypeStruct(p.shape, low) for p in row_pieces]
        + [jax.ShapeDtypeStruct(p.shape, low) for p in up_pieces]
        + [jax.ShapeDtypeStruct((total, width), low)] * 2
        + [jax.ShapeDtypeStruct((total, units), low)] * 3,
        compiler_params=pltpu.CompilerParams(vmem_limit_bytes=VMEM_MOST),
        cost_estimate=pl.CostEstimate(
            flops=48_000_000_000, bytes_accessed=60_000_000, transcendentals=2_600_000
        ),
    )(places, *row_pieces, *up_pieces, *weight_pieces, *down_pieces, spread)
    return (out[:counts], out[counts : 2 * counts]) + tuple(out[2 * counts :])


def assemble_kernel(places, *refs):
    pieces, out_ref = refs[:-1], refs[-1]
    experts_here, _, unit = out_ref.shape
    for i, piece in enumerate(pieces):

        @pl.when(pl.program_id(0) == i)
        def _():
            for j in range(experts_here):
                out_ref[j] = piece[:, j * unit : (j + 1) * unit].astype(jnp.float32)


def assemble(places, pieces, experts_here):
    rows, units = pieces[0].shape
    unit = units // experts_here
    count = len(pieces)
    return pl.pallas_call(
        assemble_kernel,
        grid_spec=pltpu.PrefetchScalarGridSpec(
            num_scalar_prefetch=1,
            grid=(count,),
            in_specs=[whole_spec(p) for p in pieces],
            out_specs=pl.BlockSpec((experts_here, rows, unit), lambda i, at: (0, 0, at[i])),
        ),
        out_shape=jax.ShapeDtypeStruct((experts_here, rows, count * unit), jnp.float32),
        compiler_params=pltpu.CompilerParams(vmem_limit_bytes=VMEM_MOST),
        cost_estimate=pl.CostEstimate(flops=0, bytes_accessed=6_000_000, transcendentals=0),
    )(places, *pieces)


X_SWAP = [(i, i ^ 1) for i in range(4)]
Y_SWAP = [(i, i ^ 2) for i in range(4)]


def core_swap(rows):
    count = lax.axis_size(SHARD)
    return lax.ppermute(rows, SHARD, [(i, i ^ 1) for i in range(count)])


def chip_send(rows, step):
    count = lax.axis_size(SHARD)
    return lax.ppermute(rows, SHARD, [(i, i ^ (2 * step)) for i in range(count)])


def x_send(rows):
    return lax.ppermute(rows, EXPERT, X_SWAP)


def y_send(rows):
    return lax.ppermute(rows, EXPERT, Y_SWAP)


def exchange(rows, split, concat):
    return lax.all_to_all(rows, SHARD, split, concat, tiled=True)


def after(values, first):
    values, _ = lax.optimization_barrier((values, first))
    return values


def add_low(a, b):
    return (a.astype(jnp.float32) + b.astype(jnp.float32)).astype(jnp.bfloat16)


def by_xor(blocks, index):
    blocks = jnp.where(index & 1, jnp.stack([blocks[1], blocks[0], blocks[3], blocks[2]]), blocks)
    return jnp.where(index & 2, jnp.stack([blocks[2], blocks[3], blocks[0], blocks[1]]), blocks)


def entry(blocks, index):
    return lax.dynamic_index_in_dim(blocks, index, 0, keepdims=False)


def chips_gather(rows):
    return [rows] + [chip_send(rows, m) for m in range(1, 4)]


def line_send(rows, pairs):
    return lax.ppermute(rows, SHARD, [(2 * a + c, 2 * b + c) for a, b in pairs for c in (0, 1)])


ACROSS = [(1, 2), (2, 1)]
OUTWARD = [(1, 0), (2, 3)]
INWARD = [(0, 1), (3, 2)]


def is_inner():
    chip = lax.axis_index(SHARD) // 2
    return (chip == 1) | (chip == 2)


def line_gather(rows):
    beside = chip_send(rows, 1)
    near, far = (line_send(r, ACROSS) for r in (rows, beside))
    near_out, far_out = (line_send(r, OUTWARD) for r in (near, far))
    inner = is_inner()
    return [rows, beside, jnp.where(inner, far, near_out), jnp.where(inner, near, far_out)]


def line_reduce(blocks):
    wide = jnp.float32
    inner = is_inner()
    from_outer = [line_send(blocks[m], INWARD) for m in (2, 3, 1)]
    near = add_low(blocks[3], from_outer[0])
    far = add_low(blocks[2], from_outer[1])
    near, far = (line_send(r, ACROSS) for r in (near, far))
    outward = line_send(add_low(blocks[1], far), OUTWARD)
    rest = jnp.where(
        inner, from_outer[2].astype(wide) + near.astype(wide), outward.astype(wide)
    )
    return blocks[0].astype(wide) + rest


def plane_gather(parts):
    block = jnp.concatenate(parts)
    half = parts[0].shape[0]
    from_x, from_y = x_send(block), y_send(block)
    far = [x_send(from_y[:half]), y_send(from_x[half:])]
    return [block, from_x, from_y] + far


def plane_reduce(blocks):
    own, to_x, to_y, far_low, far_high = blocks
    half = far_low.shape[0]
    low_part, high_part = x_send(far_low), y_send(far_high)
    to_x = jnp.concatenate([to_x[:half], add_low(to_x[half:], high_part)])
    to_y = jnp.concatenate([add_low(to_y[:half], low_part), to_y[half:]])
    from_x, from_y = x_send(to_x), y_send(to_y)
    total = own.astype(jnp.float32) + from_x.astype(jnp.float32) + from_y.astype(jnp.float32)
    total = total.astype(jnp.bfloat16)
    return total[:half], total[half:]


def local_sliced(
    inputs,
    lengths,
    routes,
    gain_attn,
    w_query,
    key_weight,
    value_weight,
    w_out,
    gain_ffn,
    w_router,
    w_gate,
    w_up,
    w_down,
    cotangent,
):
    low = jnp.bfloat16
    wide = jnp.float32
    shards = lax.axis_size(SHARD)
    expert_id, shard_id = lax.axis_index(EXPERT), lax.axis_index(SHARD)
    chip_id, core_id = shard_id // 2, shard_id % 2
    chips = shards // 2
    row_count, model_width = inputs.shape
    group_size = row_count * shards
    weight_rows = w_query.shape[0]
    query_width = w_query.shape[1] // shards
    kv_width = key_weight.shape[1] // shards
    head_width = query_width + 2 * kv_width
    packed_width = head_width + kv_width
    expert_count = w_router.shape[1]
    per_owner, slice_rows, ff = w_gate.shape
    unit = ff // chips
    unit_count = per_owner * unit
    chip_order = chip_id ^ jnp.arange(chips, dtype=jnp.int32)

    heads = query_width // HEAD_SIZE
    positions = jnp.arange(group_size, dtype=jnp.int32)
    seq_lengths = lengths[0]
    seq_ends = jnp.cumsum(seq_lengths)
    seq_starts = jnp.sum(
        jnp.where(seq_ends[None, :] <= positions[:, None], seq_lengths[None, :], 0), axis=1
    )
    offsets = (positions - seq_starts).astype(wide)
    half = HEAD_SIZE // 2
    lane = jnp.arange((heads + 1) * HEAD_SIZE)
    frequency = ROPE_BASE ** (-jnp.arange(half, dtype=wide) * 2.0 / HEAD_SIZE)
    angles = offsets[:, None] * frequency[None, :]
    cosine = jnp.tile(jnp.cos(angles), (1, 2 * (heads + 1)))
    sine = jnp.tile(jnp.sin(angles), (1, 2 * (heads + 1)))
    sine = jnp.where(lane % HEAD_SIZE < half, -sine, sine)
    start_lanes = jnp.tile(seq_starts.reshape(-1, 1, QUERY_TILE), (1, 1, heads))
    own_rows = jnp.stack(chips_gather(inputs))
    own_rows = after(own_rows, (cosine, sine, start_lanes))
    other_rows = core_swap(own_rows)
    up_chips = line_gather(cotangent)
    packed = jnp.concatenate(
        [
            w_query.reshape(weight_rows, shards, query_width),
            key_weight.reshape(weight_rows, shards, kv_width),
            value_weight.reshape(weight_rows, shards, kv_width),
            jnp.broadcast_to(gain_attn[:, None, None], (weight_rows, shards, kv_width)),
        ],
        axis=2,
    ).transpose(1, 0, 2)
    packed = exchange(packed, 0, 0).reshape(-1, packed_width)
    head_blocks = plane_gather(jnp.split(packed, 2))
    head_blocks = jnp.stack(
        [head_blocks[0], head_blocks[1], head_blocks[2], jnp.concatenate(head_blocks[3:])]
    )
    head_mat = by_xor(head_blocks, expert_id).reshape(model_width, packed_width)
    attn_gain = head_mat[:, head_width].astype(wide)

    def units_of(chip):
        pieces = [
            lax.dynamic_slice_in_dim(w, chip * unit, unit, axis=2) for w in (w_gate, w_up)
        ]
        return jnp.stack(pieces)

    own_pieces = [units_of(chip_order[m]) for m in range(chips)]
    own_pieces = own_pieces[:1] + [chip_send(own_pieces[m], m) for m in range(1, chips)]
    other_down = core_swap(w_down)

    layer_pack = jnp.concatenate(
        [
            w_out,
            w_router,
            jnp.broadcast_to(gain_ffn[:, None], (weight_rows, PAD - expert_count)),
        ],
        axis=1,
    )
    layer_chips = jnp.stack(chips_gather(layer_pack))
    layer_chips = by_xor(layer_chips, chip_id).reshape(2, 2 * weight_rows, model_width + PAD)
    layer_blocks = plane_gather([layer_chips[0], layer_chips[1]])
    layer_blocks = layer_blocks[:3] + [jnp.concatenate(layer_blocks[3:])]
    layer_mine = by_xor(jnp.stack(layer_blocks), expert_id)
    layer_theirs = core_swap(layer_mine)
    layer_cores = [
        jnp.where(core_id == c, layer_mine, layer_theirs).reshape(-1, weight_rows, model_width + PAD)
        for c in range(2)
    ]
    layer_full = jnp.stack(layer_cores, axis=1).reshape(model_width, model_width + PAD)

    group_unit, group_normed, qkv, head_attended, log_totals = attend_rows(
        jnp.concatenate([chip_order, core_id[None]]).astype(jnp.int32),
        own_rows,
        other_rows,
        head_mat,
        cosine,
        sine,
        start_lanes,
    )
    attended = exchange(head_attended, 0, 0)
    up_pieces = plane_gather(up_chips[:2]) + plane_gather(up_chips[2:])

    expert_ids = jnp.arange(PAD, dtype=jnp.int32)
    route_hits = jnp.sum((routes[:, :, None] == expert_ids).astype(wide), axis=1)
    hidden, sent_rows, router_probs = own_forward(
        attended, layer_full, inputs, route_hits, expert_count
    )
    row_chips = chips_gather(sent_rows)
    other_pieces = [core_swap(p) for p in own_pieces]
    row_pieces = plane_gather(row_chips[:2]) + plane_gather(row_chips[2:])

    unit_expert = expert_id * per_owner + jnp.arange(unit_count) // unit
    column = jnp.arange(PAD)[:, None]
    spread = ((column == unit_expert) | (column == unit_expert + expert_count)).astype(low)
    places = jnp.concatenate(
        [
            chip_order * 2 + core_id,
            chip_order * 2 + (1 - core_id),
            jnp.stack([core_id, 1 - core_id]),
        ]
    ).astype(jnp.int32)
    back_pieces, mixed_pieces, expert_in, up_rows, act_weighted, gate_grad, up_grad = experts(
        places, row_pieces, up_pieces, own_pieces + other_pieces, [w_down, other_down], spread
    )
    backs = plane_reduce(back_pieces[:5]) + plane_reduce(back_pieces[5:])
    backs = [backs[0]] + [chip_send(backs[m], m) for m in range(1, chips)]

    def share_of(part):
        parts = part.astype(low).reshape(chips, 2, slice_rows, unit_count)
        mine = lax.dynamic_index_in_dim(parts, core_id, 1, keepdims=False)
        theirs = lax.dynamic_index_in_dim(parts, 1 - core_id, 1, keepdims=False)
        total = add_low(mine, core_swap(theirs))
        pieces = [entry(total, chip_order[m]) for m in range(chips)]
        pieces = pieces[:1] + [chip_send(pieces[m], m) for m in range(1, chips)]
        return assemble(chip_order, pieces, per_owner)

    gate_part = t_mm(expert_in, gate_grad).astype(low)
    up_part = t_mm(expert_in, up_grad).astype(low)
    down_part = t_mm(act_weighted, up_rows).astype(low)
    gate_share = share_of(gate_part)
    up_share = share_of(up_part)
    down_part = down_part.reshape(per_owner, 2, unit // 2, model_width)
    down_mine = lax.dynamic_index_in_dim(down_part, core_id, 1, keepdims=False)
    down_theirs = lax.dynamic_index_in_dim(down_part, 1 - core_id, 1, keepdims=False)
    down_theirs = core_swap(down_theirs)

    hidden_grad, attended_grad, logit_grad, gain_terms = own_backward(
        backs,
        router_probs,
        route_hits,
        hidden,
        layer_full,
        cotangent,
        attended.shape,
        expert_count,
    )
    head_attended_grad = exchange(attended_grad, 0, 0)

    qkv_grad = attend_rows_back(
        qkv, head_attended, head_attended_grad, log_totals, cosine, sine, start_lanes
    )
    hidden_grad = after(hidden_grad, qkv_grad)
    layer_part = layer_grads(attended, hidden_grad, sent_rows, logit_grad, gain_terms, expert_count)
    layer_part = layer_part.reshape(4, chips, 2, weight_rows, model_width + PAD)
    layer_mine = lax.dynamic_index_in_dim(layer_part, core_id, 2, keepdims=False)
    layer_theirs = lax.dynamic_index_in_dim(layer_part, 1 - core_id, 2, keepdims=False)
    layer_sum = add_low(layer_mine, core_swap(layer_theirs))
    layer_sum = by_xor(layer_sum, expert_id).reshape(4, chips * weight_rows, model_width + PAD)
    far = jnp.split(layer_sum[3], 2)
    layer_sum = plane_reduce([layer_sum[0], layer_sum[1], layer_sum[2]] + far)
    layer_sum = jnp.concatenate(layer_sum).reshape(chips, weight_rows, model_width + PAD)
    layer_sum = by_xor(layer_sum, chip_id)
    layer_share = layer_sum[0].astype(wide) + sum(
        chip_send(layer_sum[m], m).astype(wide) for m in range(1, chips)
    )

    normed_part = mm_t(qkv_grad, head_mat)
    gain_attn_part = jnp.sum(normed_part * group_unit.astype(wide), axis=0)
    head_part = t_mm(group_normed, qkv_grad)

    mixed = plane_reduce(mixed_pieces[:5])
    mixed += plane_reduce(mixed_pieces[5:])
    output = (hidden + line_reduce(mixed)).astype(low)

    blocks = normed_part.astype(low).reshape(chips, 2, row_count, model_width)
    mine = lax.dynamic_index_in_dim(blocks, core_id, 1, keepdims=False)
    theirs = lax.dynamic_index_in_dim(blocks, 1 - core_id, 1, keepdims=False)
    summed = add_low(mine, core_swap(theirs))
    pieces = [entry(summed, chip_order[m]) for m in range(chips)]
    pieces = pieces[:1] + [chip_send(pieces[m], m) for m in range(1, chips)]
    normed_grad = sum((p.astype(wide) for p in pieces[1:]), pieces[0].astype(wide))
    down_mine = after(down_mine, normed_grad)
    down_final = down_mine.astype(wide) + down_theirs.astype(wide)
    resid = inputs.astype(wide)
    inv_attn = lax.rsqrt(jnp.mean(resid * resid, axis=-1, keepdims=True) + EPSILON)
    _, input_part = norm_back(normed_grad, resid, inv_attn, attn_gain)
    input_grad = hidden_grad + input_part

    head_pack = jnp.concatenate(
        [
            head_part[:, :head_width],
            jnp.broadcast_to(gain_attn_part[:, None], (model_width, kv_width)),
        ],
        axis=1,
    ).astype(low)
    head_blocks = by_xor(head_pack.reshape(4, model_width // 4, packed_width), expert_id)
    pair = add_low(head_blocks[:2], y_send(head_blocks[2:]))
    head_sent = x_send(pair[1])
    head_share = add_low(pair[0], head_sent)
    head_share = head_share.reshape(shards, weight_rows, packed_width)
    head_share = exchange(head_share, 0, 0).astype(wide)
    head_share = head_share.transpose(1, 0, 2)
    query_share = head_share[:, :, :query_width].reshape(weight_rows, -1)
    key_share = head_share[:, :, query_width : query_width + kv_width].reshape(weight_rows, -1)
    value_share = head_share[:, :, query_width + kv_width : head_width].reshape(weight_rows, -1)
    gain_attn_share = jnp.sum(head_share[:, :, head_width], axis=1)

    return (
        output,
        input_grad,
        gain_attn_share,
        query_share,
        key_share,
        value_share,
        layer_share[:, :model_width],
        layer_share[:, model_width + expert_count],
        layer_share[:, model_width : model_width + expert_count],
        gate_share,
        up_share,
        down_final,
    )


def solution(mesh):
    in_specs = (
        P((EXPERT, SHARD), None),
        P(EXPERT, None),
        P((EXPERT, SHARD), None),
        P((EXPERT, SHARD)),
        P((EXPERT, SHARD), None),
        P((EXPERT, SHARD), None),
        P((EXPERT, SHARD), None),
        P((EXPERT, SHARD), None),
        P((EXPERT, SHARD)),
        P((EXPERT, SHARD), None),
        P(EXPERT, SHARD, None),
        P(EXPERT, SHARD, None),
        P(EXPERT, SHARD, None),
        P((EXPERT, SHARD), None),
    )
    out_specs = (
        P((EXPERT, SHARD), None),
        P((EXPERT, SHARD), None),
        P((EXPERT, SHARD)),
        P((EXPERT, SHARD), None),
        P((EXPERT, SHARD), None),
        P((EXPERT, SHARD), None),
        P((EXPERT, SHARD), None),
        P((EXPERT, SHARD)),
        P((EXPERT, SHARD), None),
        P(EXPERT, SHARD, None),
        P(EXPERT, SHARD, None),
        P(EXPERT, SHARD, None),
    )
    if mesh.shape[SHARD] != KEY_VALUE_HEADS or mesh.shape[EXPERT] != 4:
        return jax.shard_map(
            local_gathered, mesh=mesh, in_specs=in_specs, out_specs=out_specs, check_vma=False
        )

    return jax.shard_map(local_sliced, mesh=mesh, in_specs=in_specs, out_specs=out_specs, check_vma=False)
```

```python
import functools

import jax
import jax.numpy as jnp
from jax import lax
from jax.experimental import pallas as pl
from jax.experimental.pallas import tpu as pltpu
from jax.sharding import PartitionSpec as P

SHARD = "shard"
EXPERT = "expert"
QUERY_HEADS = 24
KEY_VALUE_HEADS = 8
HEAD_SIZE = 64
SEQ_MOST = 2048
CAP = 32


EPSILON = 1e-05
SCORE_SCALE = 0.125
ROPE_BASE = 10000.0


def apply_rotation(value_rows, positions, head_count, direction_sign):
    head_width = value_rows.shape[1] // head_count
    half_width = head_width // 2
    frequency = ROPE_BASE ** (-jnp.arange(half_width, dtype=jnp.float32) * 2.0 / head_width)
    angles = positions.astype(jnp.float32)[:, None] * frequency[None, :]
    cosine = jnp.cos(angles)[:, None, :]
    sine_part = direction_sign * jnp.sin(angles)[:, None, :]
    shaped = value_rows.reshape(value_rows.shape[0], head_count, head_width)
    first_half = shaped[..., :half_width]
    second_half = shaped[..., half_width:]
    turned = jnp.concatenate(
        [
            first_half * cosine - second_half * sine_part,
            second_half * cosine + first_half * sine_part,
        ],
        axis=-1,
    )
    return turned.reshape(value_rows.shape)


def norm_rows(value_rows, gain_row):
    inv_scale = lax.rsqrt(jnp.mean(value_rows * value_rows, axis=-1, keepdims=True) + EPSILON)
    return (value_rows * inv_scale * gain_row, inv_scale)


def norm_back(norm_grad, value_rows, inv_scale, gain_row):
    gain_part = jnp.sum(norm_grad * value_rows * inv_scale, axis=0)
    scaled = norm_grad * gain_row
    value_part = inv_scale * scaled - value_rows * inv_scale**3 * jnp.mean(
        scaled * value_rows, axis=-1, keepdims=True
    )
    return (gain_part, value_part)


def split_query(value_rows):
    return value_rows.reshape(
        value_rows.shape[0], KEY_VALUE_HEADS, QUERY_HEADS // KEY_VALUE_HEADS, HEAD_SIZE
    ).transpose(1, 0, 2, 3)


def split_keys(value_rows):
    return value_rows.reshape(value_rows.shape[0], KEY_VALUE_HEADS, HEAD_SIZE).transpose(1, 0, 2)


def merge_query(value_rows):
    return value_rows.transpose(1, 0, 2, 3).reshape(value_rows.shape[1], QUERY_HEADS * HEAD_SIZE)


def merge_keys(value_rows):
    return value_rows.transpose(1, 0, 2).reshape(value_rows.shape[1], KEY_VALUE_HEADS * HEAD_SIZE)


def attend(queries, keys_win, values_win, allowed):

    def one_head(parts):
        query_head, key_head, value_head = parts
        scores = (
            jnp.einsum("tgd,wd->gtw", query_head, key_head, preferred_element_type=jnp.float32)
            * SCORE_SCALE
        )
        scores = jnp.where(allowed[None], scores, -1e30)
        largest = jnp.max(scores, axis=-1, keepdims=True)
        expo_terms = jnp.exp(scores - largest)
        totals = jnp.sum(expo_terms, axis=-1, keepdims=True)
        probs_low = (expo_terms / totals).astype(jnp.bfloat16)
        mixed_head = jnp.einsum(
            "gtw,wd->tgd", probs_low, value_head, preferred_element_type=jnp.float32
        )
        return (mixed_head.astype(jnp.bfloat16), (largest + jnp.log(totals))[..., 0])

    heads_out, log_totals = lax.map(
        one_head, (split_query(queries), split_keys(keys_win), split_keys(values_win))
    )
    return (merge_query(heads_out), log_totals)


def attend_back(queries, keys_win, values_win, outputs, out_grads, log_totals, allowed):

    def one_head(parts):
        query_head, key_head, value_head, out_head, grad_head, lse_head = parts
        scores = (
            jnp.einsum("tgd,wd->gtw", query_head, key_head, preferred_element_type=jnp.float32)
            * SCORE_SCALE
        )
        scores = jnp.where(allowed[None], scores, -1e30)
        attn_probs = jnp.exp(scores - lse_head[..., None])
        probs_low = attn_probs.astype(jnp.bfloat16)
        value_part = jnp.einsum(
            "gtw,tgd->wd", probs_low, grad_head, preferred_element_type=jnp.float32
        )
        prob_part = jnp.einsum(
            "tgd,wd->gtw", grad_head, value_head, preferred_element_type=jnp.float32
        )
        delta_rows = jnp.sum(
            out_head.astype(jnp.float32) * grad_head.astype(jnp.float32), axis=-1
        ).T
        score_grad = (attn_probs * (prob_part - delta_rows[..., None]) * SCORE_SCALE).astype(
            jnp.bfloat16
        )
        query_part = jnp.einsum(
            "gtw,wd->tgd", score_grad, key_head, preferred_element_type=jnp.float32
        )
        key_part = jnp.einsum(
            "gtw,tgd->wd", score_grad, query_head, preferred_element_type=jnp.float32
        )
        return (query_part, key_part, value_part)

    parts = (
        split_query(queries),
        split_keys(keys_win),
        split_keys(values_win),
        split_query(outputs),
        split_query(out_grads),
        log_totals,
    )
    query_parts, key_parts, value_parts = lax.map(one_head, parts)
    return (merge_query(query_parts), merge_keys(key_parts), merge_keys(value_parts))


def local_gathered(
    inputs,
    lengths,
    routes,
    gain_attn,
    w_query,
    key_weight,
    value_weight,
    w_out,
    gain_ffn,
    w_router,
    w_gate,
    w_up,
    w_down,
    cotangent,
):
    layer_full = (
        lax.all_gather(gain_attn, (EXPERT, SHARD), axis=0, tiled=True),
        lax.all_gather(w_query, (EXPERT, SHARD), axis=0, tiled=True),
        lax.all_gather(key_weight, (EXPERT, SHARD), axis=0, tiled=True),
        lax.all_gather(value_weight, (EXPERT, SHARD), axis=0, tiled=True),
        lax.all_gather(w_out, (EXPERT, SHARD), axis=0, tiled=True),
        lax.all_gather(gain_ffn, (EXPERT, SHARD), axis=0, tiled=True),
        lax.all_gather(w_router, (EXPERT, SHARD), axis=0, tiled=True),
    )
    attn_gain_low, query_mat, key_matrix, value_mat, out_mat, ffn_gain_low, router_mat = layer_full
    gate_mat, up_mat, down_mat = (
        lax.all_gather(w_gate, SHARD, axis=1, tiled=True),
        lax.all_gather(w_up, SHARD, axis=1, tiled=True),
        lax.all_gather(w_down, SHARD, axis=1, tiled=True),
    )
    attn_gain = attn_gain_low.astype(jnp.float32)
    ffn_gain = ffn_gain_low.astype(jnp.float32)
    row_count, model_width = inputs.shape
    owners = lax.axis_size(EXPERT)
    place_id = lax.axis_index(SHARD)
    group_size = row_count * lax.axis_size(SHARD)
    longest = min(SEQ_MOST, group_size // 2)
    window_size = row_count + longest
    positions = place_id * row_count + jnp.arange(row_count, dtype=jnp.int32)
    seq_lengths = lengths[0]
    seq_ends = jnp.cumsum(seq_lengths)
    seq_starts = jnp.sum(
        jnp.where(seq_ends[None, :] <= positions[:, None], seq_lengths[None, :], 0), axis=1
    )
    sequence_offsets = positions - seq_starts
    key_pos = place_id * row_count - longest + jnp.arange(window_size, dtype=jnp.int32)
    allowed = (key_pos[None, :] >= seq_starts[:, None]) & (key_pos[None, :] <= positions[:, None])
    resid = inputs.astype(jnp.float32)
    normed_wide, inv_attn = norm_rows(resid, attn_gain)
    normalized_rows = normed_wide.astype(jnp.bfloat16)
    queries = apply_rotation(
        jnp.dot(normalized_rows, query_mat, preferred_element_type=jnp.float32),
        sequence_offsets,
        QUERY_HEADS,
        1.0,
    ).astype(jnp.bfloat16)
    keys_mine = apply_rotation(
        jnp.dot(normalized_rows, key_matrix, preferred_element_type=jnp.float32),
        sequence_offsets,
        KEY_VALUE_HEADS,
        1.0,
    ).astype(jnp.bfloat16)
    values_mine = jnp.dot(normalized_rows, value_mat, preferred_element_type=jnp.float32).astype(
        jnp.bfloat16
    )
    keys_group, values_group = (
        lax.all_gather(keys_mine, SHARD, axis=0, tiled=True),
        lax.all_gather(values_mine, SHARD, axis=0, tiled=True),
    )
    kv_width = keys_mine.shape[1]
    front_pad = jnp.zeros((longest, kv_width), jnp.bfloat16)
    keys_win = lax.dynamic_slice_in_dim(
        jnp.concatenate([front_pad, keys_group], axis=0), place_id * row_count, window_size, 0
    )
    values_win = lax.dynamic_slice_in_dim(
        jnp.concatenate([front_pad, values_group], axis=0), place_id * row_count, window_size, 0
    )
    attended, log_totals = attend(queries, keys_win, values_win, allowed)
    hidden = resid + jnp.dot(attended, out_mat, preferred_element_type=jnp.float32)
    normed2_wide, inv_ffn = norm_rows(hidden, ffn_gain)
    normed2 = normed2_wide.astype(jnp.bfloat16)
    expert_count = router_mat.shape[1]
    router_probs = jax.nn.softmax(
        jnp.dot(normed2, router_mat, preferred_element_type=jnp.float32), axis=-1
    )
    top_k = routes.shape[1]
    route_hits = (
        routes[:, :, None] == jnp.arange(expert_count, dtype=jnp.int32)[None, None, :]
    ).astype(jnp.float32)
    route_weights = jnp.sum(route_hits * router_probs[:, None, :], axis=-1)
    flat_routes = routes.reshape(-1)
    flat_hits = (flat_routes[:, None] == jnp.arange(expert_count, dtype=jnp.int32)[None, :]).astype(
        jnp.int32
    )
    slot_index = jnp.sum(flat_hits * (jnp.cumsum(flat_hits, axis=0) - 1), axis=1)
    dest_index = flat_routes * CAP + slot_index
    per_owner = expert_count // owners
    exp_local = gate_mat.shape[0]
    send_rows = (
        jnp.zeros((expert_count * CAP, model_width), jnp.bfloat16)
        .at[dest_index]
        .set(jnp.repeat(normed2, top_k, axis=0))
    )
    received = lax.all_to_all(
        send_rows.reshape(owners, per_owner * CAP, model_width),
        EXPERT,
        split_axis=0,
        concat_axis=0,
        tiled=True,
    )
    received = received.reshape(owners, exp_local, CAP, model_width)
    gate_pre = jnp.einsum("sjcd,jdf->sjcf", received, gate_mat, preferred_element_type=jnp.float32)
    up_pre = jnp.einsum("sjcd,jdf->sjcf", received, up_mat, preferred_element_type=jnp.float32)
    expert_act = (jax.nn.silu(gate_pre) * up_pre).astype(jnp.bfloat16)
    expert_rows = jnp.einsum(
        "sjcf,jfd->sjcd", expert_act, down_mat, preferred_element_type=jnp.float32
    ).astype(jnp.bfloat16)
    returned = lax.all_to_all(
        expert_rows.reshape(owners, per_owner * CAP, model_width),
        EXPERT,
        split_axis=0,
        concat_axis=0,
        tiled=True,
    )
    picked = (
        returned.reshape(expert_count * CAP, model_width)[dest_index]
        .reshape(row_count, top_k, model_width)
        .astype(jnp.float32)
    )
    output = (hidden + jnp.sum(route_weights[..., None] * picked, axis=1)).astype(jnp.bfloat16)
    upstream = cotangent.astype(jnp.float32)
    weight_grads = jnp.einsum("td,tkd->tk", upstream, picked)
    rows_grad = (
        (route_weights[..., None] * upstream[:, None, :])
        .astype(jnp.bfloat16)
        .reshape(row_count * top_k, model_width)
    )
    send_grads = (
        jnp.zeros((expert_count * CAP, model_width), jnp.bfloat16).at[dest_index].set(rows_grad)
    )
    recv_grads = lax.all_to_all(
        send_grads.reshape(owners, per_owner * CAP, model_width),
        EXPERT,
        split_axis=0,
        concat_axis=0,
        tiled=True,
    )
    recv_grads = recv_grads.reshape(owners, exp_local, CAP, model_width)
    act_grad = jnp.einsum(
        "sjcd,jfd->sjcf", recv_grads, down_mat, preferred_element_type=jnp.float32
    )
    sigma = jax.nn.sigmoid(gate_pre)
    gate_pre_grad = (act_grad * up_pre * sigma * (1.0 + gate_pre * (1.0 - sigma))).astype(
        jnp.bfloat16
    )
    up_pre_grad = (act_grad * gate_pre * sigma).astype(jnp.bfloat16)
    pair_grad = (
        jnp.einsum("sjcf,jdf->sjcd", gate_pre_grad, gate_mat, preferred_element_type=jnp.float32)
        + jnp.einsum("sjcf,jdf->sjcd", up_pre_grad, up_mat, preferred_element_type=jnp.float32)
    ).astype(jnp.bfloat16)
    pair_back = lax.all_to_all(
        pair_grad.reshape(owners, per_owner * CAP, model_width),
        EXPERT,
        split_axis=0,
        concat_axis=0,
        tiled=True,
    )
    normed2_grad = jnp.sum(
        pair_back.reshape(expert_count * CAP, model_width)[dest_index]
        .reshape(row_count, top_k, model_width)
        .astype(jnp.float32),
        axis=1,
    )
    down_part = jnp.einsum(
        "sjcf,sjcd->jfd", expert_act, recv_grads, preferred_element_type=jnp.float32
    )
    gate_part = jnp.einsum(
        "sjcd,sjcf->jdf", received, gate_pre_grad, preferred_element_type=jnp.float32
    )
    up_part = jnp.einsum(
        "sjcd,sjcf->jdf", received, up_pre_grad, preferred_element_type=jnp.float32
    )
    gate_share, up_share, down_final = (
        lax.psum_scatter(
            gate_part.astype(jnp.bfloat16), SHARD, scatter_dimension=1, tiled=True
        ).astype(jnp.float32),
        lax.psum_scatter(
            up_part.astype(jnp.bfloat16), SHARD, scatter_dimension=1, tiled=True
        ).astype(jnp.float32),
        lax.psum_scatter(
            down_part.astype(jnp.bfloat16), SHARD, scatter_dimension=1, tiled=True
        ).astype(jnp.float32),
    )
    prob_grad = jnp.sum(route_hits * weight_grads[..., None], axis=1)
    logit_grad = (
        router_probs * (prob_grad - jnp.sum(router_probs * prob_grad, axis=-1, keepdims=True))
    ).astype(jnp.bfloat16)
    router_part = jnp.dot(normed2.T, logit_grad, preferred_element_type=jnp.float32)
    normed2_grad = normed2_grad + jnp.dot(
        logit_grad, router_mat.T, preferred_element_type=jnp.float32
    )
    gain_ffn_part, hidden_part = norm_back(normed2_grad, hidden, inv_ffn, ffn_gain)
    hidden_grad = upstream + hidden_part
    hidden_low = hidden_grad.astype(jnp.bfloat16)
    out_part = jnp.dot(attended.T, hidden_low, preferred_element_type=jnp.float32)
    attended_grad = jnp.dot(hidden_low, out_mat.T, preferred_element_type=jnp.float32).astype(
        jnp.bfloat16
    )
    query_raw, keys_part, values_part = attend_back(
        queries, keys_win, values_win, attended, attended_grad, log_totals, allowed
    )
    spread_zero = jnp.zeros((longest + group_size, kv_width), jnp.float32)
    keys_spread = lax.dynamic_update_slice_in_dim(spread_zero, keys_part, place_id * row_count, 0)[
        longest:
    ]
    values_spread = lax.dynamic_update_slice_in_dim(
        spread_zero, values_part, place_id * row_count, 0
    )[longest:]
    keys_unrotated, values_raw = (
        lax.psum_scatter(keys_spread, SHARD, scatter_dimension=0, tiled=True),
        lax.psum_scatter(values_spread, SHARD, scatter_dimension=0, tiled=True),
    )
    queries_grad = apply_rotation(query_raw, sequence_offsets, QUERY_HEADS, -1.0).astype(
        jnp.bfloat16
    )
    keys_gradient = apply_rotation(keys_unrotated, sequence_offsets, KEY_VALUE_HEADS, -1.0).astype(
        jnp.bfloat16
    )
    values_grad = values_raw.astype(jnp.bfloat16)
    query_part = jnp.dot(normalized_rows.T, queries_grad, preferred_element_type=jnp.float32)
    key_part = jnp.dot(normalized_rows.T, keys_gradient, preferred_element_type=jnp.float32)
    value_part = jnp.dot(normalized_rows.T, values_grad, preferred_element_type=jnp.float32)
    normed_grad = (
        jnp.dot(queries_grad, query_mat.T, preferred_element_type=jnp.float32)
        + jnp.dot(keys_gradient, key_matrix.T, preferred_element_type=jnp.float32)
        + jnp.dot(values_grad, value_mat.T, preferred_element_type=jnp.float32)
    )
    gain_attn_part, input_part = norm_back(normed_grad, resid, inv_attn, attn_gain)
    input_grad = hidden_grad + input_part
    layer_grads = (
        lax.psum_scatter(gain_attn_part, (EXPERT, SHARD), scatter_dimension=0, tiled=True),
        lax.psum_scatter(query_part, (EXPERT, SHARD), scatter_dimension=0, tiled=True),
        lax.psum_scatter(key_part, (EXPERT, SHARD), scatter_dimension=0, tiled=True),
        lax.psum_scatter(value_part, (EXPERT, SHARD), scatter_dimension=0, tiled=True),
        lax.psum_scatter(out_part, (EXPERT, SHARD), scatter_dimension=0, tiled=True),
        lax.psum_scatter(gain_ffn_part, (EXPERT, SHARD), scatter_dimension=0, tiled=True),
        lax.psum_scatter(router_part, (EXPERT, SHARD), scatter_dimension=0, tiled=True),
    )
    return (
        output,
        input_grad,
        layer_grads[0],
        layer_grads[1],
        layer_grads[2],
        layer_grads[3],
        layer_grads[4],
        layer_grads[5],
        layer_grads[6],
        gate_share,
        up_share,
        down_final,
    )


VMEM_MOST = 60 * 1024 * 1024
ROW_TILE = 256
QUERY_TILE = 256
PAD = 128


def mm(a, b):
    return jnp.dot(a, b, preferred_element_type=jnp.float32)


def mm_t(a, b):
    return lax.dot_general(a, b, (((1,), (1,)), ((), ())), preferred_element_type=jnp.float32)


def t_mm(a, b):
    return lax.dot_general(a, b, (((0,), (0,)), ((), ())), preferred_element_type=jnp.float32)


def lane_row(rows, lane):
    lanes = lax.broadcasted_iota(jnp.int32, (8, rows.shape[1]), 1)
    return mm_t((lanes == lane).astype(rows.dtype), rows)[:1]


def tile_spec(rows, cols):
    return pl.BlockSpec((rows, cols), lambda i, *_: (i, 0))


def whole_spec(array):
    zeros = (0,) * len(array.shape)
    return pl.BlockSpec(array.shape, lambda *_: zeros, pipeline_mode=pl.Buffered(1))


def turn(rows, cosine, sine):
    lane = lax.broadcasted_iota(jnp.int32, rows.shape, 1)
    width = rows.shape[1]
    half = HEAD_SIZE // 2
    other = jnp.where(
        lane % HEAD_SIZE < half, pltpu.roll(rows, width - half, 1), pltpu.roll(rows, half, 1)
    )
    return rows * cosine + other * sine


def stacked(rows, heads):
    return jnp.concatenate(
        [rows[:, h * HEAD_SIZE : (h + 1) * HEAD_SIZE] for h in range(heads)], axis=0
    )


def side_by_side(rows, heads):
    count = rows.shape[0] // heads
    return jnp.concatenate([rows[h * count : (h + 1) * count] for h in range(heads)], axis=1)


def head_lanes(ref, heads):
    return jnp.concatenate(
        [
            ref[d, h * HEAD_SIZE : (h + 1) * HEAD_SIZE, :]
            for h in range(heads)
            for d in range(ref.shape[0])
        ],
        axis=1,
    )


def scores_of(keys, queries, start_row, step):
    scores = mm_t(keys, queries) * SCORE_SCALE
    key_pos = lax.broadcasted_iota(jnp.int32, scores.shape, 0)
    lane = lax.broadcasted_iota(jnp.int32, (1, scores.shape[1]), 1)
    query_pos = step * QUERY_TILE + lane % QUERY_TILE
    allowed = (key_pos >= start_row) & (key_pos <= query_pos)
    return jnp.where(allowed, scores, -1e30)


def tiles_of(ref):
    return ref.shape[0] // QUERY_TILE


def attend_kernel(
    heads,
    places,
    own_ref,
    other_ref,
    mat_ref,
    cos_ref,
    sin_ref,
    start_ref,
    unit_ref,
    normed_ref,
    qkv_ref,
    out_ref,
    lse_ref,
    keys_all,
    values_all,
    gain_row,
):
    step = pl.program_id(0)
    low, wide = jnp.bfloat16, jnp.float32
    query_width = heads * HEAD_SIZE
    turned_width = query_width + HEAD_SIZE

    @pl.when(step == 0)
    def _():
        keys_all[...] = jnp.zeros_like(keys_all)
        values_all[...] = jnp.zeros_like(values_all)
        gain_row[...] = lane_row(mat_ref[:, turned_width:], HEAD_SIZE)

    own, other = own_ref[0].astype(wide), other_ref[0].astype(wide)
    first = places[tiles_of(keys_all)] == 0
    x = jnp.concatenate([jnp.where(first, own, other), jnp.where(first, other, own)], axis=0)
    scaled = x * lax.rsqrt(jnp.mean(x * x, axis=-1, keepdims=True) + EPSILON)
    unit_ref[...] = scaled.astype(low)
    normed = (scaled * gain_row[...]).astype(low)
    normed_ref[...] = normed
    projected = mm(normed, mat_ref[...])
    turned = turn(projected[:, :turned_width], cos_ref[...], sin_ref[...]).astype(low)
    values = projected[:, turned_width:].astype(low)
    qkv_ref[:, :turned_width] = turned
    qkv_ref[:, turned_width:] = values
    here = pl.ds(pl.multiple_of(step * QUERY_TILE, QUERY_TILE), QUERY_TILE)
    keys_all[here, :] = turned[:, query_width:]
    values_all[here, :] = values[:, :HEAD_SIZE]
    queries = stacked(turned[:, :query_width], heads)
    scores = scores_of(keys_all[...], queries, start_ref[0], step)
    largest = jnp.max(scores, axis=0, keepdims=True)
    terms = jnp.exp(scores - largest)
    totals = jnp.sum(terms, axis=0, keepdims=True)
    probs = (terms / totals).astype(low)
    mixed = t_mm(values_all[...], probs).astype(low)
    blocks, _, block_rows = out_ref.shape
    for h in range(heads):
        for d in range(blocks):
            first_lane = h * QUERY_TILE + d * block_rows
            out_ref[d, h * HEAD_SIZE : (h + 1) * HEAD_SIZE, :] = mixed[
                :, first_lane : first_lane + block_rows
            ]
    lse_ref[0] = largest + jnp.log(totals)


def attend_rows(places, own_rows, other_rows, mat, cosine, sine, starts):
    low = jnp.bfloat16
    tiles, part, width = own_rows.shape
    rows = tiles * QUERY_TILE
    packed = mat.shape[1]
    heads = packed // HEAD_SIZE - 3
    lanes = pl.BlockSpec((1, 1, heads * QUERY_TILE), lambda i, _: (i, 0, 0))
    turned_width = (heads + 1) * HEAD_SIZE
    return pl.pallas_call(
        functools.partial(attend_kernel, heads),
        grid_spec=pltpu.PrefetchScalarGridSpec(
            num_scalar_prefetch=1,
            grid=(tiles,),
            in_specs=[
                pl.BlockSpec((1, part, width), lambda i, at: (at[i], 0, 0)),
                pl.BlockSpec((1, part, width), lambda i, at: (at[i], 0, 0)),
                whole_spec(mat),
                tile_spec(QUERY_TILE, turned_width),
                tile_spec(QUERY_TILE, turned_width),
                lanes,
            ],
            out_specs=[
                tile_spec(QUERY_TILE, width),
                tile_spec(QUERY_TILE, width),
                tile_spec(QUERY_TILE, packed),
                pl.BlockSpec((QUERY_TILE // part, heads * HEAD_SIZE, part), lambda i, _: (i, 0, 0)),
                lanes,
            ],
            scratch_shapes=[
                pltpu.VMEM((rows, HEAD_SIZE), low),
                pltpu.VMEM((rows, HEAD_SIZE), low),
                pltpu.VMEM((1, width), jnp.float32),
            ],
        ),
        out_shape=[
            jax.ShapeDtypeStruct((rows, width), low),
            jax.ShapeDtypeStruct((rows, width), low),
            jax.ShapeDtypeStruct((rows, packed), low),
            jax.ShapeDtypeStruct((rows // part, heads * HEAD_SIZE, part), low),
            jax.ShapeDtypeStruct((tiles, 1, heads * QUERY_TILE), jnp.float32),
        ],
        compiler_params=pltpu.CompilerParams(vmem_limit_bytes=VMEM_MOST),
        cost_estimate=pl.CostEstimate(
            flops=9_000_000_000, bytes_accessed=20_000_000, transcendentals=3_000_000
        ),
    )(places, own_rows, other_rows, mat, cosine, sine, starts)


def attend_back_kernel(
    heads,
    qkv_ref,
    out_ref,
    grad_ref,
    lse_ref,
    cos_ref,
    sin_ref,
    start_ref,
    grads_ref,
    keys_acc,
    values_acc,
    queries_grad,
):
    step = pl.program_id(0)
    low, wide = jnp.bfloat16, jnp.float32
    query_width = heads * HEAD_SIZE
    turned_width = query_width + HEAD_SIZE

    @pl.when(step == 0)
    def _():
        keys_acc[...] = jnp.zeros_like(keys_acc)
        values_acc[...] = jnp.zeros_like(values_acc)

    here = pl.ds(pl.multiple_of(step * QUERY_TILE, QUERY_TILE), QUERY_TILE)
    keys = qkv_ref[:, query_width:turned_width]
    values = qkv_ref[:, turned_width : turned_width + HEAD_SIZE]
    queries = stacked(qkv_ref[here, :query_width], heads)
    grads = head_lanes(grad_ref, heads)
    outs = head_lanes(out_ref, heads)
    delta = jnp.sum(outs.astype(wide) * grads.astype(wide), axis=0, keepdims=True)
    scores = scores_of(keys, queries, start_ref[0], step)
    probs = jnp.exp(scores - lse_ref[0])
    values_acc[...] += mm_t(probs.astype(low), grads)
    score_grad = (probs * (mm(values, grads) - delta) * SCORE_SCALE).astype(low)
    keys_acc[...] += mm(score_grad, queries)
    queries_grad[here, :] = side_by_side(t_mm(keys, score_grad).T, heads)

    @pl.when(step == pl.num_programs(0) - 1)
    def _():
        both = jnp.concatenate([queries_grad[...], keys_acc[...]], axis=1)
        grads_ref[:, :turned_width] = turn(both, cos_ref[...], -sin_ref[...]).astype(low)
        grads_ref[:, turned_width:] = jnp.concatenate(
            [values_acc[...].astype(low), jnp.zeros(values_acc.shape, low)], axis=1
        )


def attend_rows_back(qkv, out, grad, lse, cosine, sine, starts):
    rows, packed = qkv.shape
    heads = packed // HEAD_SIZE - 3
    tiles = rows // QUERY_TILE
    lanes = pl.BlockSpec((1, 1, heads * QUERY_TILE), lambda i: (i, 0, 0))
    part = out.shape[2]
    blocks = pl.BlockSpec((QUERY_TILE // part, heads * HEAD_SIZE, part), lambda i: (i, 0, 0))
    return pl.pallas_call(
        functools.partial(attend_back_kernel, heads),
        grid=(tiles,),
        in_specs=[
            whole_spec(qkv),
            blocks,
            blocks,
            lanes,
            whole_spec(cosine),
            whole_spec(sine),
            lanes,
        ],
        out_specs=pl.BlockSpec((rows, packed), lambda i: (0, 0)),
        out_shape=jax.ShapeDtypeStruct((rows, packed), jnp.bfloat16),
        scratch_shapes=[
            pltpu.VMEM((rows, HEAD_SIZE), jnp.float32),
            pltpu.VMEM((rows, HEAD_SIZE), jnp.float32),
            pltpu.VMEM((rows, heads * HEAD_SIZE), jnp.float32),
        ],
        compiler_params=pltpu.CompilerParams(vmem_limit_bytes=VMEM_MOST),
        cost_estimate=pl.CostEstimate(
            flops=10_000_000_000, bytes_accessed=20_000_000, transcendentals=3_000_000
        ),
    )(qkv, out, grad, lse, cosine, sine, starts)


def own_forward_kernel(
    expert_count, attended_ref, layer_ref, x_ref, hits_ref, hidden_ref, sent_ref, probs_ref
):
    low, wide = jnp.bfloat16, jnp.float32
    width = x_ref.shape[1]
    attended = attended_ref[...].reshape(width, attended_ref.shape[2])
    hidden = x_ref[...].astype(wide) + t_mm(attended, layer_ref[:, :width])
    hidden_ref[...] = hidden
    inv = lax.rsqrt(jnp.mean(hidden * hidden, axis=-1, keepdims=True) + EPSILON)
    normed = (hidden * inv * lane_row(layer_ref[:, width:], expert_count)).astype(low)
    sent_ref[:, :width] = normed
    logits = mm(normed, layer_ref[:, width:])
    lane = lax.broadcasted_iota(jnp.int32, logits.shape, 1)
    logits = jnp.where(lane < expert_count, logits, -1e30)
    terms = jnp.exp(logits - jnp.max(logits, axis=-1, keepdims=True))
    probs = terms / jnp.sum(terms, axis=-1, keepdims=True)
    probs_ref[...] = probs
    weights = probs * hits_ref[...]
    high = weights.astype(low).astype(wide)
    rest = pltpu.roll(weights - high, expert_count, 1)
    sent_ref[:, width:] = (high + rest).astype(low)


def own_forward(attended, layer_full, x, hits, expert_count):
    rows, width = x.shape
    return pl.pallas_call(
        functools.partial(own_forward_kernel, expert_count),
        out_shape=[
            jax.ShapeDtypeStruct((rows, width), jnp.float32),
            jax.ShapeDtypeStruct((rows, width + PAD), jnp.bfloat16),
            jax.ShapeDtypeStruct((rows, PAD), jnp.float32),
        ],
        compiler_params=pltpu.CompilerParams(vmem_limit_bytes=VMEM_MOST),
        cost_estimate=pl.CostEstimate(
            flops=3_000_000_000, bytes_accessed=10_000_000, transcendentals=20_000
        ),
    )(attended, layer_full, x, hits)


def own_backward_kernel(
    expert_count,
    back0_ref,
    back1_ref,
    back2_ref,
    back3_ref,
    probs_ref,
    hits_ref,
    hidden_ref,
    layer_ref,
    up_ref,
    grad_ref,
    attended_grad_ref,
    logit_ref,
    gain_ref,
):
    low, wide = jnp.bfloat16, jnp.float32
    width = up_ref.shape[1]
    total = back0_ref[...].astype(wide) + back1_ref[...].astype(wide)
    total += back2_ref[...].astype(wide) + back3_ref[...].astype(wide)
    probs = probs_ref[...]
    prob_grad = total[:, width:] * hits_ref[...]
    logit_grad = probs * (prob_grad - jnp.sum(probs * prob_grad, axis=-1, keepdims=True))
    logit_low = logit_grad.astype(low)
    logit_ref[...] = logit_low
    normed_grad = total[:, :width] + mm_t(logit_low, layer_ref[:, width:])
    hidden = hidden_ref[...]
    inv = lax.rsqrt(jnp.mean(hidden * hidden, axis=-1, keepdims=True) + EPSILON)
    gain_ref[...] = (normed_grad * hidden * inv).astype(low)
    scaled = normed_grad * lane_row(layer_ref[:, width:], expert_count)
    hidden_part = inv * scaled - hidden * inv * inv * inv * jnp.mean(
        scaled * hidden, axis=-1, keepdims=True
    )
    hidden_grad = up_ref[...].astype(wide) + hidden_part
    grad_ref[...] = hidden_grad
    attended_grad = mm_t(layer_ref[:, :width], hidden_grad.astype(low)).astype(low)
    attended_grad_ref[...] = attended_grad.reshape(attended_grad_ref.shape)


def own_backward(backs, probs, hits, hidden, layer_full, cotangent, heads_shape, expert_count):
    rows, width = cotangent.shape
    low = jnp.bfloat16
    return pl.pallas_call(
        functools.partial(own_backward_kernel, expert_count),
        out_shape=[
            jax.ShapeDtypeStruct((rows, width), jnp.float32),
            jax.ShapeDtypeStruct(heads_shape, low),
            jax.ShapeDtypeStruct((rows, PAD), low),
            jax.ShapeDtypeStruct((rows, width), low),
        ],
        compiler_params=pltpu.CompilerParams(vmem_limit_bytes=VMEM_MOST),
        cost_estimate=pl.CostEstimate(
            flops=3_000_000_000, bytes_accessed=10_000_000, transcendentals=1_000
        ),
    )(*backs, probs, hits, hidden, layer_full, cotangent)


def layer_grads_kernel(
    expert_count, attended_ref, grad_ref, sent_ref, logit_ref, gain_ref, out_ref
):
    low = jnp.bfloat16
    width = grad_ref.shape[1]
    attended = attended_ref[...].reshape(width, attended_ref.shape[2])
    out_ref[:, :width] = mm(attended, grad_ref[...].astype(low)).astype(low)
    lane = lax.broadcasted_iota(jnp.int32, logit_ref.shape, 1)
    ones = (lane == expert_count).astype(low)
    tail = t_mm(sent_ref[:, :width], logit_ref[...]) + t_mm(gain_ref[...], ones)
    out_ref[:, width:] = tail.astype(low)


def layer_grads(attended, hidden_grad, sent_rows, logit_grad, gain_terms, expert_count):
    width = hidden_grad.shape[1]
    return pl.pallas_call(
        functools.partial(layer_grads_kernel, expert_count),
        out_shape=jax.ShapeDtypeStruct((width, width + PAD), jnp.bfloat16),
        compiler_params=pltpu.CompilerParams(vmem_limit_bytes=VMEM_MOST),
        cost_estimate=pl.CostEstimate(
            flops=3_000_000_000, bytes_accessed=8_000_000, transcendentals=0
        ),
    )(attended, hidden_grad, sent_rows, logit_grad, gain_terms)


def tile_parts(pieces):
    half = ROW_TILE // 2
    parts = [p.at[i * half : (i + 1) * half] for p in pieces for i in range(p.shape[0] // half)]
    return [parts[i : i + 2] for i in range(0, len(parts), 2)]


def expert_kernel(counts, *refs):
    places, refs = refs[0], refs[1:]

    def take(count):
        nonlocal refs
        taken, refs = refs[:count], refs[count:]
        return taken

    row_refs, up_refs = take(counts), take(counts)
    weight_refs, down_refs, (spread_ref,) = take(8), take(2), take(1)
    back_refs, mix_refs = take(counts), take(counts)
    rows_out, ups_out, act_ref, gate_grad_ref, up_grad_ref = take(5)
    gate_mat, up_mat, down_mat, rows, ups, backs, mixes = take(7)
    back_acc, mix_acc, cols_acc, weight_sems, in_sems, out_sems = refs
    low = jnp.bfloat16
    step, steps = pl.program_id(0), pl.num_programs(0)
    slot = lax.rem(step, 2)
    experts_here, width, unit = gate_mat.shape
    slice_rows = weight_refs[0].shape[2]
    half = ROW_TILE // 2
    halves = (slice(0, half), slice(half, ROW_TILE))
    sources = list(zip(tile_parts(row_refs), tile_parts(up_refs)))
    targets = list(zip(tile_parts(back_refs), tile_parts(mix_refs)))

    def weight_copies():
        for p, piece in enumerate(weight_refs):
            at = pl.ds(pl.multiple_of(places[p] * slice_rows, slice_rows), slice_rows)
            for t, mat in enumerate((gate_mat, up_mat)):
                yield pltpu.make_async_copy(
                    piece.at[t], mat.at[:, at, :], weight_sems.at[2 * p + t]
                )
        share = down_refs[0].shape[1]
        for p, piece in enumerate(down_refs):
            at = pl.ds(pl.multiple_of(places[8 + p] * share, share), share)
            yield pltpu.make_async_copy(piece, down_mat.at[:, at, :], weight_sems.at[16 + p])

    def tile_in(tile, at):
        for h in range(2):
            for i, (parts, held) in enumerate(zip(sources[tile], (rows, ups))):
                yield pltpu.make_async_copy(
                    parts[h], held.at[at, halves[h]], in_sems.at[at, 2 * h + i]
                )

    def tile_out(tile, at):
        for h in range(2):
            for i, (parts, held) in enumerate(zip(targets[tile], (backs, mixes))):
                yield pltpu.make_async_copy(
                    held.at[at, halves[h]], parts[h], out_sems.at[at, 2 * h + i]
                )

    @pl.when(step == 0)
    def _():
        for copy in tile_in(0, 0):
            copy.start()
        for copy in weight_copies():
            copy.start()

    for tile in range(1, len(sources)):

        @pl.when(step + 1 == tile)
        def _():
            for copy in tile_in(tile, tile % 2):
                copy.start()

    for copy in tile_in(0, slot):
        copy.wait()

    @pl.when(step == 0)
    def _():
        for copy in weight_copies():
            copy.wait()

    x = rows[slot, :, :width]
    weights = rows[slot, :, width:]
    u = ups[slot]
    rows_out[...] = x
    ups_out[...] = u
    pair = 2
    for c in range(experts_here // pair):
        at = slice(c * pair * unit, (c + 1) * pair * unit)
        both = slice(c * pair, (c + 1) * pair)
        gate_here = jnp.concatenate([gate_mat[c * pair + i] for i in range(pair)], axis=1)
        up_here = jnp.concatenate([up_mat[c * pair + i] for i in range(pair)], axis=1)
        down_here = down_mat[both].reshape(pair * unit, width)
        gate_pre = mm(x, gate_here)
        up_pre = mm(x, up_here)
        down_back = mm_t(u, down_here)
        pair_weight = mm(weights, spread_ref[:, at])
        sigma = jax.nn.sigmoid(gate_pre)
        gated = gate_pre * sigma
        act = gated * up_pre
        act_low = (act * pair_weight).astype(low)
        terms = (act * down_back).astype(low)
        act_grad = pair_weight * down_back
        gate_low = (act_grad * up_pre * (sigma + gated * (1.0 - sigma))).astype(low)
        up_low = (act_grad * gated).astype(low)
        act_ref[:, at] = act_low
        gate_grad_ref[:, at] = gate_low
        up_grad_ref[:, at] = up_low
        back = mm_t(gate_low, gate_here) + mm_t(up_low, up_here)
        mixed = mm(act_low, down_here)
        cols = mm_t(terms, spread_ref[:, at])
        if c == 0:
            back_acc[...] = back
            mix_acc[...] = mixed
            cols_acc[...] = cols
        else:
            back_acc[...] += back
            mix_acc[...] += mixed
            cols_acc[...] += cols

    @pl.when(step >= 2)
    def _():
        for copy in tile_out(0, slot):
            copy.wait()

    backs[slot, :, :width] = back_acc[...].astype(low)
    backs[slot, :, width:] = cols_acc[...].astype(low)
    mixes[slot] = mix_acc[...].astype(low)
    for tile in range(len(targets)):

        @pl.when(step == tile)
        def _():
            for copy in tile_out(tile, tile % 2):
                copy.start()

    @pl.when(step == steps - 1)
    def _():
        for copy in tile_out(0, 1 - slot):
            copy.wait()
        for copy in tile_out(0, slot):
            copy.wait()


def experts(places, row_pieces, up_pieces, weight_pieces, down_pieces, spread):
    low, wide = jnp.bfloat16, jnp.float32
    width = up_pieces[0].shape[1]
    padded = row_pieces[0].shape[1]
    experts_here = down_pieces[0].shape[0]
    units = spread.shape[1]
    unit = units // experts_here
    total = sum(p.shape[0] for p in row_pieces)
    counts = len(row_pieces)
    anywhere = pl.BlockSpec(memory_space=pl.ANY)
    out = pl.pallas_call(
        functools.partial(expert_kernel, counts),
        grid_spec=pltpu.PrefetchScalarGridSpec(
            num_scalar_prefetch=1,
            grid=(total // ROW_TILE,),
            in_specs=[anywhere] * (2 * counts + 10) + [whole_spec(spread)],
            out_specs=[anywhere] * (2 * counts)
            + [tile_spec(ROW_TILE, width)] * 2
            + [tile_spec(ROW_TILE, units)] * 3,
            scratch_shapes=[
                pltpu.VMEM((experts_here, width, unit), low),
                pltpu.VMEM((experts_here, width, unit), low),
                pltpu.VMEM((experts_here, unit, width), low),
                pltpu.VMEM((2, ROW_TILE, padded), low),
                pltpu.VMEM((2, ROW_TILE, width), low),
                pltpu.VMEM((2, ROW_TILE, padded), low),
                pltpu.VMEM((2, ROW_TILE, width), low),
                pltpu.VMEM((ROW_TILE, width), wide),
                pltpu.VMEM((ROW_TILE, width), wide),
                pltpu.VMEM((ROW_TILE, padded - width), wide),
                pltpu.SemaphoreType.DMA((18,)),
                pltpu.SemaphoreType.DMA((2, 4)),
                pltpu.SemaphoreType.DMA((2, 4)),
            ],
        ),
        out_shape=[jax.ShapeDtypeStruct(p.shape, low) for p in row_pieces]
        + [jax.ShapeDtypeStruct(p.shape, low) for p in up_pieces]
        + [jax.ShapeDtypeStruct((total, width), low)] * 2
        + [jax.ShapeDtypeStruct((total, units), low)] * 3,
        compiler_params=pltpu.CompilerParams(vmem_limit_bytes=VMEM_MOST),
        cost_estimate=pl.CostEstimate(
            flops=48_000_000_000, bytes_accessed=60_000_000, transcendentals=2_600_000
        ),
    )(places, *row_pieces, *up_pieces, *weight_pieces, *down_pieces, spread)
    return (out[:counts], out[counts : 2 * counts]) + tuple(out[2 * counts :])


def assemble_kernel(places, *refs):
    pieces, out_ref = refs[:-1], refs[-1]
    experts_here, _, unit = out_ref.shape
    for i, piece in enumerate(pieces):

        @pl.when(pl.program_id(0) == i)
        def _():
            for j in range(experts_here):
                out_ref[j] = piece[:, j * unit : (j + 1) * unit].astype(jnp.float32)


def assemble(places, pieces, experts_here):
    rows, units = pieces[0].shape
    unit = units // experts_here
    count = len(pieces)
    return pl.pallas_call(
        assemble_kernel,
        grid_spec=pltpu.PrefetchScalarGridSpec(
            num_scalar_prefetch=1,
            grid=(count,),
            in_specs=[whole_spec(p) for p in pieces],
            out_specs=pl.BlockSpec((experts_here, rows, unit), lambda i, at: (0, 0, at[i])),
        ),
        out_shape=jax.ShapeDtypeStruct((experts_here, rows, count * unit), jnp.float32),
        compiler_params=pltpu.CompilerParams(vmem_limit_bytes=VMEM_MOST),
        cost_estimate=pl.CostEstimate(flops=0, bytes_accessed=6_000_000, transcendentals=0),
    )(places, *pieces)


X_SWAP = [(i, i ^ 1) for i in range(4)]
Y_SWAP = [(i, i ^ 2) for i in range(4)]


def core_swap(rows):
    count = lax.axis_size(SHARD)
    return lax.ppermute(rows, SHARD, [(i, i ^ 1) for i in range(count)])


def chip_send(rows, step):
    count = lax.axis_size(SHARD)
    return lax.ppermute(rows, SHARD, [(i, i ^ (2 * step)) for i in range(count)])


def x_send(rows):
    return lax.ppermute(rows, EXPERT, X_SWAP)


def y_send(rows):
    return lax.ppermute(rows, EXPERT, Y_SWAP)


def exchange(rows, split, concat):
    return lax.all_to_all(rows, SHARD, split, concat, tiled=True)


def after(values, first):
    values, _ = lax.optimization_barrier((values, first))
    return values


def add_low(a, b):
    return (a.astype(jnp.float32) + b.astype(jnp.float32)).astype(jnp.bfloat16)


def by_xor(blocks, index):
    blocks = jnp.where(index & 1, jnp.stack([blocks[1], blocks[0], blocks[3], blocks[2]]), blocks)
    return jnp.where(index & 2, jnp.stack([blocks[2], blocks[3], blocks[0], blocks[1]]), blocks)


def entry(blocks, index):
    return lax.dynamic_index_in_dim(blocks, index, 0, keepdims=False)


def chips_gather(rows):
    return [rows] + [chip_send(rows, m) for m in range(1, 4)]


def line_send(rows, pairs):
    return lax.ppermute(rows, SHARD, [(2 * a + c, 2 * b + c) for a, b in pairs for c in (0, 1)])


ACROSS = [(1, 2), (2, 1)]
OUTWARD = [(1, 0), (2, 3)]
INWARD = [(0, 1), (3, 2)]


def is_inner():
    chip = lax.axis_index(SHARD) // 2
    return (chip == 1) | (chip == 2)


def line_gather(rows):
    beside = chip_send(rows, 1)
    near, far = (line_send(r, ACROSS) for r in (rows, beside))
    near_out, far_out = (line_send(r, OUTWARD) for r in (near, far))
    inner = is_inner()
    return [rows, beside, jnp.where(inner, far, near_out), jnp.where(inner, near, far_out)]


def line_reduce(blocks):
    wide = jnp.float32
    inner = is_inner()
    from_outer = [line_send(blocks[m], INWARD) for m in (2, 3, 1)]
    near = add_low(blocks[3], from_outer[0])
    far = add_low(blocks[2], from_outer[1])
    near, far = (line_send(r, ACROSS) for r in (near, far))
    outward = line_send(add_low(blocks[1], far), OUTWARD)
    rest = jnp.where(
        inner, from_outer[2].astype(wide) + near.astype(wide), outward.astype(wide)
    )
    return blocks[0].astype(wide) + rest


def plane_gather(parts):
    block = jnp.concatenate(parts)
    half = parts[0].shape[0]
    from_x, from_y = x_send(block), y_send(block)
    far = [x_send(from_y[:half]), y_send(from_x[half:])]
    return [block, from_x, from_y] + far


def plane_reduce(blocks, first=None):
    own, to_x, to_y, far_low, far_high = blocks
    half = far_low.shape[0]
    low_part, high_part = x_send(far_low), y_send(far_high)
    if first is not None:
        low_part, high_part = after((low_part, high_part), first)
    to_x = jnp.concatenate([to_x[:half], add_low(to_x[half:], high_part)])
    to_y = jnp.concatenate([add_low(to_y[:half], low_part), to_y[half:]])
    from_x, from_y = x_send(to_x), y_send(to_y)
    total = own.astype(jnp.float32) + from_x.astype(jnp.float32) + from_y.astype(jnp.float32)
    total = total.astype(jnp.bfloat16)
    return total[:half], total[half:]


def local_sliced(
    inputs,
    lengths,
    routes,
    gain_attn,
    w_query,
    key_weight,
    value_weight,
    w_out,
    gain_ffn,
    w_router,
    w_gate,
    w_up,
    w_down,
    cotangent,
):
    low = jnp.bfloat16
    wide = jnp.float32
    shards = lax.axis_size(SHARD)
    expert_id, shard_id = lax.axis_index(EXPERT), lax.axis_index(SHARD)
    chip_id, core_id = shard_id // 2, shard_id % 2
    chips = shards // 2
    row_count, model_width = inputs.shape
    group_size = row_count * shards
    weight_rows = w_query.shape[0]
    query_width = w_query.shape[1] // shards
    kv_width = key_weight.shape[1] // shards
    head_width = query_width + 2 * kv_width
    packed_width = head_width + kv_width
    expert_count = w_router.shape[1]
    per_owner, slice_rows, ff = w_gate.shape
    unit = ff // chips
    unit_count = per_owner * unit
    chip_order = chip_id ^ jnp.arange(chips, dtype=jnp.int32)

    heads = query_width // HEAD_SIZE
    positions = jnp.arange(group_size, dtype=jnp.int32)
    seq_lengths = lengths[0]
    seq_ends = jnp.cumsum(seq_lengths)
    seq_starts = jnp.sum(
        jnp.where(seq_ends[None, :] <= positions[:, None], seq_lengths[None, :], 0), axis=1
    )
    offsets = (positions - seq_starts).astype(wide)
    half = HEAD_SIZE // 2
    lane = jnp.arange((heads + 1) * HEAD_SIZE)
    frequency = ROPE_BASE ** (-jnp.arange(half, dtype=wide) * 2.0 / HEAD_SIZE)
    angles = offsets[:, None] * frequency[None, :]
    cosine = jnp.tile(jnp.cos(angles), (1, 2 * (heads + 1)))
    sine = jnp.tile(jnp.sin(angles), (1, 2 * (heads + 1)))
    sine = jnp.where(lane % HEAD_SIZE < half, -sine, sine)
    start_lanes = jnp.tile(seq_starts.reshape(-1, 1, QUERY_TILE), (1, 1, heads))
    own_rows = jnp.stack(chips_gather(inputs))
    own_rows = after(own_rows, (cosine, sine, start_lanes))
    other_rows = core_swap(own_rows)
    up_chips = line_gather(cotangent)
    packed = jnp.concatenate(
        [
            w_query.reshape(weight_rows, shards, query_width),
            key_weight.reshape(weight_rows, shards, kv_width),
            value_weight.reshape(weight_rows, shards, kv_width),
            jnp.broadcast_to(gain_attn[:, None, None], (weight_rows, shards, kv_width)),
        ],
        axis=2,
    ).transpose(1, 0, 2)
    packed = exchange(packed, 0, 0).reshape(-1, packed_width)
    head_blocks = plane_gather(jnp.split(packed, 2))
    head_blocks = jnp.stack(
        [head_blocks[0], head_blocks[1], head_blocks[2], jnp.concatenate(head_blocks[3:])]
    )
    head_mat = by_xor(head_blocks, expert_id).reshape(model_width, packed_width)
    attn_gain = head_mat[:, head_width].astype(wide)

    def units_of(chip):
        pieces = [
            lax.dynamic_slice_in_dim(w, chip * unit, unit, axis=2) for w in (w_gate, w_up)
        ]
        return jnp.stack(pieces)

    own_pieces = [units_of(chip_order[m]) for m in range(chips)]
    own_pieces = own_pieces[:1] + [chip_send(own_pieces[m], m) for m in range(1, chips)]
    other_down = core_swap(w_down)

    layer_pack = jnp.concatenate(
        [
            w_out,
            w_router,
            jnp.broadcast_to(gain_ffn[:, None], (weight_rows, PAD - expert_count)),
        ],
        axis=1,
    )
    layer_chips = jnp.stack(chips_gather(layer_pack))
    layer_chips = by_xor(layer_chips, chip_id).reshape(2, 2 * weight_rows, model_width + PAD)
    layer_blocks = plane_gather([layer_chips[0], layer_chips[1]])
    layer_blocks = layer_blocks[:3] + [jnp.concatenate(layer_blocks[3:])]
    layer_mine = by_xor(jnp.stack(layer_blocks), expert_id)
    layer_theirs = core_swap(layer_mine)
    layer_cores = [
        jnp.where(core_id == c, layer_mine, layer_theirs).reshape(-1, weight_rows, model_width + PAD)
        for c in range(2)
    ]
    layer_full = jnp.stack(layer_cores, axis=1).reshape(model_width, model_width + PAD)

    group_unit, group_normed, qkv, head_attended, log_totals = attend_rows(
        jnp.concatenate([chip_order, core_id[None]]).astype(jnp.int32),
        own_rows,
        other_rows,
        head_mat,
        cosine,
        sine,
        start_lanes,
    )
    attended = exchange(head_attended, 0, 0)
    up_pieces = plane_gather(up_chips[:2]) + plane_gather(up_chips[2:])

    expert_ids = jnp.arange(PAD, dtype=jnp.int32)
    route_hits = jnp.sum((routes[:, :, None] == expert_ids).astype(wide), axis=1)
    hidden, sent_rows, router_probs = own_forward(
        attended, layer_full, inputs, route_hits, expert_count
    )
    row_chips = chips_gather(sent_rows)
    other_pieces = [core_swap(p) for p in own_pieces]
    row_pieces = plane_gather(row_chips[:2]) + plane_gather(row_chips[2:])

    unit_expert = expert_id * per_owner + jnp.arange(unit_count) // unit
    column = jnp.arange(PAD)[:, None]
    spread = ((column == unit_expert) | (column == unit_expert + expert_count)).astype(low)
    places = jnp.concatenate(
        [
            chip_order * 2 + core_id,
            chip_order * 2 + (1 - core_id),
            jnp.stack([core_id, 1 - core_id]),
        ]
    ).astype(jnp.int32)
    back_pieces, mixed_pieces, expert_in, up_rows, act_weighted, gate_grad, up_grad = experts(
        places, row_pieces, up_pieces, own_pieces + other_pieces, [w_down, other_down], spread
    )
    backs = plane_reduce(back_pieces[:5]) + plane_reduce(back_pieces[5:])
    backs = [backs[0]] + [chip_send(backs[m], m) for m in range(1, chips)]

    def share_of(part):
        parts = part.astype(low).reshape(chips, 2, slice_rows, unit_count)
        mine = lax.dynamic_index_in_dim(parts, core_id, 1, keepdims=False)
        theirs = lax.dynamic_index_in_dim(parts, 1 - core_id, 1, keepdims=False)
        total = add_low(mine, core_swap(theirs))
        pieces = [entry(total, chip_order[m]) for m in range(chips)]
        pieces = pieces[:1] + [chip_send(pieces[m], m) for m in range(1, chips)]
        return assemble(chip_order, pieces, per_owner)

    gate_part = t_mm(expert_in, gate_grad).astype(low)
    up_part = t_mm(expert_in, up_grad).astype(low)
    down_part = t_mm(act_weighted, up_rows).astype(low)
    gate_share = share_of(gate_part)
    up_share = share_of(up_part)
    down_part = down_part.reshape(per_owner, 2, unit // 2, model_width)
    down_mine = lax.dynamic_index_in_dim(down_part, core_id, 1, keepdims=False)
    down_theirs = lax.dynamic_index_in_dim(down_part, 1 - core_id, 1, keepdims=False)
    down_theirs = core_swap(down_theirs)

    hidden_grad, attended_grad, logit_grad, gain_terms = own_backward(
        backs,
        router_probs,
        route_hits,
        hidden,
        layer_full,
        cotangent,
        attended.shape,
        expert_count,
    )
    head_attended_grad = exchange(attended_grad, 0, 0)

    qkv_grad = attend_rows_back(
        qkv, head_attended, head_attended_grad, log_totals, cosine, sine, start_lanes
    )
    hidden_grad = after(hidden_grad, qkv_grad)
    layer_part = layer_grads(attended, hidden_grad, sent_rows, logit_grad, gain_terms, expert_count)
    layer_part = layer_part.reshape(4, chips, 2, weight_rows, model_width + PAD)
    layer_mine = lax.dynamic_index_in_dim(layer_part, core_id, 2, keepdims=False)
    layer_theirs = lax.dynamic_index_in_dim(layer_part, 1 - core_id, 2, keepdims=False)
    layer_sum = add_low(layer_mine, core_swap(layer_theirs))
    layer_sum = by_xor(layer_sum, expert_id).reshape(4, chips * weight_rows, model_width + PAD)
    far = jnp.split(layer_sum[3], 2)
    layer_sum = plane_reduce([layer_sum[0], layer_sum[1], layer_sum[2]] + far)
    layer_sum = jnp.concatenate(layer_sum).reshape(chips, weight_rows, model_width + PAD)
    layer_sum = by_xor(layer_sum, chip_id)
    layer_share = layer_sum[0].astype(wide) + sum(
        chip_send(layer_sum[m], m).astype(wide) for m in range(1, chips)
    )

    normed_part = mm_t(qkv_grad, head_mat)
    gain_attn_part = jnp.sum(normed_part * group_unit.astype(wide), axis=0)
    head_part = t_mm(group_normed, qkv_grad)

    blocks = normed_part.astype(low).reshape(chips, 2, row_count, model_width)
    mine = lax.dynamic_index_in_dim(blocks, core_id, 1, keepdims=False)
    theirs = lax.dynamic_index_in_dim(blocks, 1 - core_id, 1, keepdims=False)
    summed = add_low(mine, core_swap(theirs))
    mixed = plane_reduce(mixed_pieces[:5], summed)
    mixed += plane_reduce(mixed_pieces[5:], summed)
    output = (hidden + line_reduce(mixed)).astype(low)

    pieces = [entry(summed, chip_order[m]) for m in range(chips)]
    pieces = pieces[:1] + [chip_send(pieces[m], m) for m in range(1, chips)]
    normed_grad = sum((p.astype(wide) for p in pieces[1:]), pieces[0].astype(wide))
    down_mine = after(down_mine, normed_grad)
    down_final = down_mine.astype(wide) + down_theirs.astype(wide)
    resid = inputs.astype(wide)
    inv_attn = lax.rsqrt(jnp.mean(resid * resid, axis=-1, keepdims=True) + EPSILON)
    _, input_part = norm_back(normed_grad, resid, inv_attn, attn_gain)
    input_grad = hidden_grad + input_part

    head_pack = jnp.concatenate(
        [
            head_part[:, :head_width],
            jnp.broadcast_to(gain_attn_part[:, None], (model_width, kv_width)),
        ],
        axis=1,
    ).astype(low)
    head_blocks = by_xor(head_pack.reshape(4, model_width // 4, packed_width), expert_id)
    pair = add_low(head_blocks[:2], y_send(head_blocks[2:]))
    head_sent = x_send(pair[1])
    head_share = add_low(pair[0], head_sent)
    head_share = head_share.reshape(shards, weight_rows, packed_width)
    head_share = exchange(head_share, 0, 0).astype(wide)
    head_share = head_share.transpose(1, 0, 2)
    query_share = head_share[:, :, :query_width].reshape(weight_rows, -1)
    key_share = head_share[:, :, query_width : query_width + kv_width].reshape(weight_rows, -1)
    value_share = head_share[:, :, query_width + kv_width : head_width].reshape(weight_rows, -1)
    gain_attn_share = jnp.sum(head_share[:, :, head_width], axis=1)

    return (
        output,
        input_grad,
        gain_attn_share,
        query_share,
        key_share,
        value_share,
        layer_share[:, :model_width],
        layer_share[:, model_width + expert_count],
        layer_share[:, model_width : model_width + expert_count],
        gate_share,
        up_share,
        down_final,
    )


def solution(mesh):
    in_specs = (
        P((EXPERT, SHARD), None),
        P(EXPERT, None),
        P((EXPERT, SHARD), None),
        P((EXPERT, SHARD)),
        P((EXPERT, SHARD), None),
        P((EXPERT, SHARD), None),
        P((EXPERT, SHARD), None),
        P((EXPERT, SHARD), None),
        P((EXPERT, SHARD)),
        P((EXPERT, SHARD), None),
        P(EXPERT, SHARD, None),
        P(EXPERT, SHARD, None),
        P(EXPERT, SHARD, None),
        P((EXPERT, SHARD), None),
    )
    out_specs = (
        P((EXPERT, SHARD), None),
        P((EXPERT, SHARD), None),
        P((EXPERT, SHARD)),
        P((EXPERT, SHARD), None),
        P((EXPERT, SHARD), None),
        P((EXPERT, SHARD), None),
        P((EXPERT, SHARD), None),
        P((EXPERT, SHARD)),
        P((EXPERT, SHARD), None),
        P(EXPERT, SHARD, None),
        P(EXPERT, SHARD, None),
        P(EXPERT, SHARD, None),
    )
    if mesh.shape[SHARD] != KEY_VALUE_HEADS or mesh.shape[EXPERT] != 4:
        return jax.shard_map(
            local_gathered, mesh=mesh, in_specs=in_specs, out_specs=out_specs, check_vma=False
        )

    return jax.shard_map(local_sliced, mesh=mesh, in_specs=in_specs, out_specs=out_specs, check_vma=False)
```
